256 devices in a mesh: span: 16 (over y, z_lo, core), seq: 16 (over z_hi, x).
Axes of the slice: x: 4, y: 4, z: 8 (z_hi: 4, z_lo: 2; z = z_hi * 2 + z_lo), core: 2. Of those that a mesh axis runs over, the one named last changes fastest.
Arguments:
- query: bfloat16 [16, 2048, 48, 128], P('span', 'seq'), may hold values from -8 to 8
- keys: bfloat16 [16, 2048, 48, 128], P('span', 'seq'), may hold values from -6 to 6
- values: bfloat16 [16, 2048, 48, 128], P('span', 'seq'), may hold values from -6 to 6
- block_list: int32 [16, 16, 32], P('span'), may hold values from 0 to 31, as said below
- block_count: int32 [16, 16], P('span'), may hold values from 1 to 32
Outputs:
- attended: bfloat16 [16, 2048, 48, 128], P('span', 'seq')
The draws below stay inside these ranges and needn't reach their ends.
Inputs may be any that keep to these rules, and one draw needn't show every extreme that they name: `block_list`: each row names every one of the 32 tiles once; the used slots of query tile t name exactly the own tiles 16 to 16 + t and, for spans after the first, some of the previous span's tiles (none for span 0); slots at or after block_count are not used.
All inputs are finite; a program needn't handle non-finite values.
Results may differ from the reference program's by a relative error of at most 0.005.
Values may be sent and summed in bfloat16 or wider, within the bound.
A program may use at most 128 MiB of HBM per device.

```python
import math
import jax
import jax.numpy as jnp
from jax import lax

H = 48
HD = 128
CTOK = 2048
CTILES = 16
SPANS = 16


def draw_query(key, part):
    shape = (SPANS, CTOK, H, HD)
    drawn = jnp.clip(jax.random.normal(jax.random.fold_in(key, 1), shape, jnp.float32), -6.0, 6.0)
    return drawn.astype(jnp.bfloat16)


def draw_keys(key, part):
    shape = (SPANS, CTOK, H, HD)
    drawn = jnp.clip(jax.random.normal(jax.random.fold_in(key, 2), shape, jnp.float32), -6.0, 6.0)
    return drawn.astype(jnp.bfloat16)


def tile_plan(key):
    noise = jax.random.randint(jax.random.fold_in(key, 3), (SPANS, CTILES, CTILES), 0, 2 ** 20)
    tiles = jnp.arange(CTILES, dtype=jnp.int32)
    ranking = noise * CTILES + tiles[None, None, :]
    earlier_order = lax.top_k(ranking, CTILES)[1].astype(jnp.int32)
    dropped = jax.random.randint(jax.random.fold_in(key, 4), (SPANS, CTILES), 0, CTILES // 4 + 1)
    dropped = jnp.where(tiles[None, :] == CTILES - 1, 0, dropped)
    span_ids = jnp.arange(SPANS, dtype=jnp.int32)
    kept_count = jnp.where(span_ids[:, None] == 0, 0, CTILES - dropped).astype(jnp.int32)
    counts = (kept_count + tiles[None, :] + 1).astype(jnp.int32)
    return (earlier_order, kept_count, counts)


def draw_block_list(key, part):
    earlier_order, kept_count, counts = tile_plan(key)
    tiles = jnp.arange(CTILES, dtype=jnp.int32)
    kept = kept_count[:, :, None]
    earlier_rank = jnp.where(tiles[None, None, :] < kept, tiles[None, None, :], 2 * CTILES + tiles[None, None, :])
    query_tile = tiles[None, :, None]
    own_rank = jnp.where(tiles[None, None, :] <= query_tile, kept + tiles[None, None, :], 3 * CTILES + tiles[None, None, :])
    own_tiles = jnp.broadcast_to(CTILES + tiles[None, None, :], (SPANS, CTILES, CTILES))
    candidates = jnp.concatenate([earlier_order, own_tiles], -1)
    sort_keys = jnp.concatenate([earlier_rank, own_rank], -1).astype(jnp.int32)
    placing = jnp.argsort(sort_keys, axis=-1, stable=True)
    return jnp.take_along_axis(candidates, placing, axis=-1).astype(jnp.int32)


def draw_block_count(key, part):
    earlier_order, kept_count, counts = tile_plan(key)
    return counts


def steps_of(key, shape, split, low, top_value):
    gain = 1.0
    for dim, blocks in split:
        heights = jax.random.uniform(jax.random.fold_in(jax.random.fold_in(key, 6), dim), (blocks,), jnp.float32, low / len(split), top_value / len(split))
        gain = gain * jnp.repeat(jnp.exp(heights), shape[dim] // blocks).reshape((-1,) + (1,) * (len(shape) - 1 - dim))
    return gain


def gaussian(stream_key, extent, spread, bound, cuts=(), kind=jnp.bfloat16):
    loudness = steps_of(stream_key, extent, cuts, -0.22, 0.18) if cuts else 1.0
    values = jax.random.normal(stream_key, extent, jnp.float32) * spread * loudness
    return jnp.minimum(jnp.maximum(values, -bound), bound).astype(kind)


def setup_inputs(seed: int = 0) -> dict:
    arg_keys = jax.random.split(jax.random.key(seed), 6)
    return {
        "query": draw_query(jax.random.fold_in(arg_keys[5], 71), 0),
        "keys": draw_keys(jax.random.fold_in(arg_keys[5], 71), 0),
        "values": gaussian(arg_keys[2], (SPANS, CTOK, H, HD), 1.0, 6.0, ((0, 16), (1, 16))),
        "block_list": draw_block_list(jax.random.fold_in(arg_keys[5], 71), 0),
        "block_count": draw_block_count(jax.random.fold_in(arg_keys[5], 71), 0),
    }


def visible_tiles(tile_lists, tile_counts):
    pool_count = tile_lists.shape[1]
    slots = jnp.arange(pool_count, dtype=jnp.int32)
    used = slots[None, :] < tile_counts[:, None]
    named = (tile_lists[:, :, None] == slots[None, None, :]) & used[:, :, None]
    return jnp.any(named, axis=1)

def attend_span(query, keys, values, earlier_keys, earlier_values, tile_lists, tile_counts):
    tile_count = tile_lists.shape[0]
    tile_rows = query.shape[0] // tile_count
    head_count = query.shape[1]
    head_width = query.shape[2]
    pool_keys = jnp.concatenate([earlier_keys, keys], 0).astype(jnp.float32)
    pool_values = jnp.concatenate([earlier_values, values], 0).astype(jnp.float32)
    seen = visible_tiles(tile_lists, tile_counts)
    key_tile = jnp.arange(2 * tile_count * tile_rows, dtype=jnp.int32) // tile_rows
    score_scale = 1.0 / math.sqrt(head_width)
    query_tiles = query.reshape(tile_count, tile_rows, head_count, head_width)

    def one_tile(item):
        query_tile, seen_row = item
        scores = jnp.einsum('qhd,khd->hqk', query_tile.astype(jnp.float32), pool_keys, precision=lax.Precision.HIGHEST) * score_scale
        visible = seen_row[key_tile]
        masked = jnp.where(visible[None, None, :], scores, -jnp.inf)
        largest = lax.optimization_barrier(jnp.max(masked, axis=-1, keepdims=True))
        weights = jnp.where(visible[None, None, :], jnp.exp(masked - largest), 0.0)
        summed = lax.optimization_barrier(jnp.sum(weights, axis=-1, keepdims=True))
        weights_bf = (weights / summed).astype(jnp.bfloat16)
        result = jnp.einsum('hqk,khd->qhd', weights_bf.astype(jnp.float32), pool_values, precision=lax.Precision.HIGHEST)
        return result.astype(jnp.bfloat16)
    return lax.map(one_tile, (query_tiles, seen)).reshape(query.shape)

def reference(query, keys, values, block_list, block_count):

    def per_span(span_index):
        earlier = jnp.maximum(span_index - 1, 0)
        return attend_span(query[span_index], keys[span_index], values[span_index], keys[earlier], values[earlier], block_list[span_index], block_count[span_index])
    return lax.map(per_span, jnp.arange(SPANS, dtype=jnp.int32))
```

```python
import functools
import math

import jax
import jax.numpy as jnp
from jax import lax
from jax.experimental import pallas as pl
from jax.experimental.pallas import tpu as pltpu
from jax.sharding import PartitionSpec as P

MESH = pl.DeviceIdType.MESH
TILE = 128
TILES = 16
TOKENS = TILE * TILES
SPANS = 16
SEQ = 16
HEADS = 48
PER = HEADS // SEQ
WIDTH = 128
QB = 512
KB = 1024
SCALE = math.log2(math.e) / math.sqrt(WIDTH)
HIDDEN = -1e30
CONTRACT_LAST = (((1,), (1,)), ((), ()))
CONTRACT_FIRST = (((0,), (0,)), ((), ()))
CONTRACT_PLAIN = (((1,), (0,)), ((), ()))


def worker_of(span):
    return (span % 8) // 2 * 4 + span // 8 * 2 + span % 2


def span_of(index):
    return (index // 2) % 2 * 8 + index // 4 * 2 + index % 2


def matmul(left, right, dims):
    return lax.dot_general(left, right, dims, preferred_element_type=jnp.float32)


def kernel(
    q_in, k_in, v_in, vis_in, o_out,
    qb, kb, vb, ob, vis, bias, scores,
    in_send, in_recv, vis_send, vis_recv, fwd_send, fwd_recv, o_send, o_recv,
):
    me_span = lax.axis_index("span")
    me_seq = lax.axis_index("seq")
    span = span_of(me_span)
    target = worker_of(me_span)
    after = worker_of(lax.rem(span + 1, SPANS))
    home_works = target == me_span

    ins = (q_in, k_in, v_in)

    def landing(which, head, tile):
        rows = pl.ds(pl.multiple_of(tile * TILE, TILE), TILE)
        own = pl.ds(pl.multiple_of(TOKENS + tile * TILE, TILE), TILE)
        if which == 0:
            return qb.at[head, rows, :]
        if which == 1:
            return kb.at[head, own, :]
        return vb.at[head, :, own]

    def landed(which, head):
        if which == 0:
            return qb.at[head]
        if which == 1:
            return kb.at[head, TOKENS:, :]
        return vb.at[head, :, TOKENS:]

    def peer(step):
        return lax.rem(me_seq + step, SEQ)

    def send_block(which, head, to):
        return pltpu.make_async_remote_copy(
            src_ref=ins[which].at[to * PER + head],
            dst_ref=landing(which, head, me_seq),
            send_sem=in_send.at[which, head],
            recv_sem=in_recv.at[which, head],
            device_id=(target, to),
            device_id_type=MESH,
        )

    def send_vis(to):
        return pltpu.make_async_remote_copy(
            src_ref=vis_in, dst_ref=vis, send_sem=vis_send, recv_sem=vis_recv,
            device_id=(target, to), device_id_type=MESH,
        )

    def send_out(head, tile, to):
        return pltpu.make_async_remote_copy(
            src_ref=ob.at[head, pl.ds(pl.multiple_of(tile * TILE, TILE), TILE), :],
            dst_ref=o_out.at[me_seq * PER + head],
            send_sem=o_send, recv_sem=o_recv,
            device_id=(span, to), device_id_type=MESH,
        )

    def forward(which, head, part):
        rows = pl.ds(part * 512, 512)
        own = pl.ds(TOKENS + part * 512, 512)
        if which == 1:
            src, dst = kb.at[head, own, :], kb.at[head, rows, :]
        else:
            src, dst = vb.at[head, :, own], vb.at[head, :, rows]
        return pltpu.make_async_remote_copy(
            src_ref=src, dst_ref=dst,
            send_sem=fwd_send.at[which - 1, head], recv_sem=fwd_recv.at[which - 1, head],
            device_id=(after, me_seq), device_id_type=MESH,
        )

    @pl.when(span == 0)
    def _():
        kb[:, :TOKENS, :] = jnp.zeros((PER, TOKENS, WIDTH), jnp.bfloat16)
        vb[:, :, :TOKENS] = jnp.zeros((PER, WIDTH, TOKENS), jnp.bfloat16)

    @pl.when(home_works)
    def _():
        pltpu.make_async_copy(vis_in, vis, vis_recv).start()

    @pl.when(jnp.logical_not(home_works))
    def _():
        send_vis(me_seq).start()

    for head in range(PER):
        for which in (1, 2, 0):
            @pl.loop(1, SEQ)
            def _(step):
                send_block(which, head, peer(step)).start()

            @pl.when(home_works)
            def _():
                pltpu.make_async_copy(
                    ins[which].at[me_seq * PER + head],
                    landing(which, head, me_seq),
                    in_recv.at[which, head],
                ).start()

            @pl.when(jnp.logical_not(home_works))
            def _():
                send_block(which, head, me_seq).start()

    pltpu.make_async_copy(vis, vis, vis_recv).wait()
    tile_of = lax.broadcasted_iota(jnp.int32, (TILE, TOKENS), 1) // TILE
    pick = (tile_of == lax.broadcasted_iota(jnp.int32, (TILE, TOKENS), 0)).astype(jnp.bfloat16)
    seen = matmul(vis[...].astype(jnp.bfloat16), pick, CONTRACT_PLAIN)
    bias[...] = (1.0 - seen) * HIDDEN

    for head in range(PER):
        for which in (1, 2):
            pltpu.make_async_copy(
                landed(which, head), landed(which, head), in_recv.at[which, head]
            ).wait()

            @pl.when(span != SPANS - 1)
            def _():
                for part in range(4):
                    forward(which, head, part).start()

        pltpu.make_async_copy(landed(0, head), landed(0, head), in_recv.at[0, head]).wait()

        @pl.when(span != 0)
        def _():
            for which, prev in ((1, kb.at[head, :TOKENS, :]), (2, vb.at[head, :, :TOKENS])):
                pltpu.make_async_copy(prev, prev, fwd_recv.at[which - 1, head]).wait()

        @pl.loop(0, TOKENS // QB)
        def _(block):
            start = pl.multiple_of(block * QB, QB)
            columns = pl.ds(start, QB)
            query = qb[head, columns, :]
            chunks = TOKENS // KB + (block * QB + QB + KB - 1) // KB

            def score(chunk, largest):
                first = pl.multiple_of(chunk * KB, KB)
                part = matmul(kb[head, pl.ds(first, KB), :], query, CONTRACT_LAST)
                scores[pl.ds(first, KB), :] = part
                for tile in range(KB // TILE):
                    rows = part[tile * TILE:(tile + 1) * TILE].reshape(TILE // 8, 8, QB)
                    hidden = bias[pl.ds(chunk * (KB // TILE) + tile, 1), columns]
                    largest = jnp.maximum(largest, jnp.max(rows, axis=0) + hidden)
                return largest

            largest = lax.fori_loop(0, chunks, score, jnp.full((8, QB), -3e38, jnp.float32))
            top = jnp.max(largest, axis=0, keepdims=True) * SCALE

            def weigh(chunk, carry):
                total, summed = carry
                first = pl.multiple_of(chunk * KB, KB)
                parts = []
                for tile in range(KB // TILE):
                    hidden = bias[pl.ds(chunk * (KB // TILE) + tile, 1), columns]
                    rows = scores[pl.ds(first + tile * TILE, TILE), :]
                    weight = jnp.exp2(rows * SCALE - (top - hidden))
                    summed = summed + jnp.sum(weight.reshape(TILE // 8, 8, QB), axis=0)
                    parts.append(weight.astype(jnp.bfloat16))
                weights = jnp.concatenate(parts, 0)
                total = total + matmul(vb[head, :, pl.ds(first, KB)], weights, CONTRACT_PLAIN)
                return total, summed

            total, summed = lax.fori_loop(
                0, chunks, weigh,
                (jnp.zeros((WIDTH, QB), jnp.float32), jnp.zeros((8, QB), jnp.float32)),
            )
            result = total / jnp.sum(summed, axis=0, keepdims=True)
            ob[head, columns, :] = jnp.transpose(result).astype(jnp.bfloat16)

            for part in range(QB // TILE):
                tile = block * (QB // TILE) + part
                here = jnp.logical_and(span == me_span, tile == me_seq)

                @pl.when(here)
                def _():
                    pltpu.make_async_copy(
                        ob.at[head, pl.ds(pl.multiple_of(tile * TILE, TILE), TILE), :],
                        o_out.at[me_seq * PER + head],
                        o_recv,
                    ).start()

                @pl.when(jnp.logical_not(here))
                def _():
                    send_out(head, tile, tile).start()

    pltpu.make_async_copy(o_out, o_out, o_recv).wait()

    for head in range(PER):
        for which in (0, 1, 2):
            sent = ins[which].at[: SEQ - 1]
            pltpu.make_async_copy(sent, sent, in_send.at[which, head]).wait()

            @pl.when(jnp.logical_not(home_works))
            def _():
                send_block(which, head, me_seq).wait_send()

        @pl.when(span != SPANS - 1)
        def _():
            for which, own in ((1, kb.at[head, TOKENS:, :]), (2, vb.at[head, :, TOKENS:])):
                pltpu.make_async_copy(own, own, fwd_send.at[which - 1, head]).wait()

    @pl.when(jnp.logical_not(home_works))
    def _():
        send_vis(me_seq).wait_send()

    sent = o_out.at[: HEADS - PER]
    pltpu.make_async_copy(sent, sent, o_send).wait()

    @pl.when(span != me_span)
    def _():
        last = o_out.at[:PER]
        pltpu.make_async_copy(last, last, o_send).wait()


def exchange_and_attend(query, keys, values, visible):
    anywhere = pl.BlockSpec(memory_space=pl.ANY)
    return pl.pallas_call(
        kernel,
        out_shape=jax.ShapeDtypeStruct((HEADS, TILE, WIDTH), jnp.bfloat16),
        in_specs=[anywhere] * 4,
        out_specs=anywhere,
        scratch_shapes=[
            pltpu.VMEM((PER, TOKENS, WIDTH), jnp.bfloat16),
            pltpu.VMEM((PER, 2 * TOKENS, WIDTH), jnp.bfloat16),
            pltpu.VMEM((PER, WIDTH, 2 * TOKENS), jnp.bfloat16),
            pltpu.VMEM((PER, TOKENS, WIDTH), jnp.bfloat16),
            pltpu.VMEM((2 * TILES, TILE), jnp.float32),
            pltpu.VMEM((2 * TILES, TOKENS), jnp.float32),
            pltpu.VMEM((2 * TOKENS, QB), jnp.float32),
            pltpu.SemaphoreType.DMA((3, PER)),
            pltpu.SemaphoreType.DMA((3, PER)),
            pltpu.SemaphoreType.DMA,
            pltpu.SemaphoreType.DMA,
            pltpu.SemaphoreType.DMA((2, PER)),
            pltpu.SemaphoreType.DMA((2, PER)),
            pltpu.SemaphoreType.DMA,
            pltpu.SemaphoreType.DMA,
        ],
        compiler_params=pltpu.CompilerParams(
            vmem_limit_bytes=56 << 20, has_side_effects=True
        ),
        name="exchange_and_attend",
    )(query, keys, values, visible)


def visible_tiles(tile_lists, tile_counts):
    slots = jnp.arange(2 * TILES, dtype=jnp.int32)
    used = slots[None, :] < tile_counts[:, None]
    named = (tile_lists[:, :, None] == slots[None, None, :]) & used[:, :, None]
    return jnp.any(named, axis=1).T.astype(jnp.float32)


def per_device(query, keys, values, block_list, block_count):
    visible = jnp.pad(
        visible_tiles(block_list[0], block_count[0]), ((0, 0), (0, TILE - TILES))
    )
    result = exchange_and_attend(
        jnp.transpose(query[0], (1, 0, 2)),
        jnp.transpose(keys[0], (1, 0, 2)),
        jnp.transpose(values[0], (1, 2, 0)),
        visible,
    )
    return jnp.transpose(result, (1, 0, 2))[None]


def solution(mesh):
    in_specs = (
        P("span", "seq", None, None),
        P("span", "seq", None, None),
        P("span", "seq", None, None),
        P("span", None, None),
        P("span", None),
    )
    out_specs = P("span", "seq", None, None)
    return jax.shard_map(
        per_device, mesh=mesh, in_specs=in_specs, out_specs=out_specs, check_vma=False
    )
```

```python
import functools
import math

import jax
import jax.numpy as jnp
from jax import lax
from jax.experimental import pallas as pl
from jax.experimental.pallas import tpu as pltpu
from jax.sharding import PartitionSpec as P

MESH = pl.DeviceIdType.MESH
TILE = 128
TILES = 16
TOKENS = TILE * TILES
SPANS = 16
SEQ = 16
HEADS = 48
PER = HEADS // SEQ
WIDTH = 128
QB = 512
KB = 1024
SCALE = math.log2(math.e) / math.sqrt(WIDTH)
HIDDEN = -1e30
CONTRACT_LAST = (((1,), (1,)), ((), ()))
CONTRACT_FIRST = (((0,), (0,)), ((), ()))
CONTRACT_PLAIN = (((1,), (0,)), ((), ()))


def matmul(left, right, dims):
    return lax.dot_general(left, right, dims, preferred_element_type=jnp.float32)


def kernel(
    q_in, k_in, v_in, vis_in, o_out,
    qb, kb, vb, ob, vis, bias, scores,
    in_send, in_recv, vis_send, vis_recv, fwd_send, fwd_recv, o_send, o_recv,
):
    me_span = lax.axis_index("span")
    me_seq = lax.axis_index("seq")
    row = me_span // 4
    local = lax.rem(me_span, 4)
    core = lax.rem(me_span, 2)
    plane = lax.rem(me_span // 2, 2)
    x = lax.rem(me_seq, 4)
    side = lax.rem(x, 2)
    z = me_seq // 4 * 2 + plane
    me_group = x // 2 * 8 + z
    item_spans = (2 * core, 2 * core + 1, 2 * side + core)
    item_heads = (3 * me_group + side, 3 * me_group + side, 3 * me_group + 2)

    ins = (q_in, k_in, v_in)
    base = (0, 1, 3)

    def place(which, slot, tile):
        at = pl.ds(pl.multiple_of(slot * TOKENS + tile * TILE, TILE), TILE)
        if which == 0:
            return qb.at[at, :]
        if which == 1:
            return kb.at[at, :]
        return vb.at[:, at]

    def slot_ref(which, slot):
        at = pl.ds(slot * TOKENS, TOKENS)
        if which == 0:
            return qb.at[at, :]
        if which == 1:
            return kb.at[at, :]
        return vb.at[:, at]

    def item_slot(which, item):
        return item if which == 0 else base[item] + 1

    def chip(group, x_side, its_core):
        its_z = lax.rem(group, 8)
        return (
            row * 4 + lax.rem(its_z, 2) * 2 + its_core,
            its_z // 2 * 4 + group // 8 * 2 + x_side,
        )

    def major_block(which, step, x_side):
        group = lax.rem(me_group + step, 16)
        item = lax.rem(local, 2)
        slot = item if which == 0 else 1 + item
        return pltpu.make_async_remote_copy(
            src_ref=ins[which].at[3 * group + x_side],
            dst_ref=place(which, slot, me_seq),
            send_sem=in_send.at[which, 0], recv_sem=in_recv.at[which, item],
            device_id=chip(group, x_side, local // 2), device_id_type=MESH,
        )

    def shared_block(which, step):
        group = lax.rem(me_group + step, 16)
        return pltpu.make_async_remote_copy(
            src_ref=ins[which].at[3 * group + 2],
            dst_ref=place(which, item_slot(which, 2), me_seq),
            send_sem=in_send.at[which, 1], recv_sem=in_recv.at[which, 2],
            device_id=chip(group, local // 2, lax.rem(local, 2)), device_id_type=MESH,
        )

    major_home = local // 2 == core
    shared_home = local // 2 == side

    def start_major(which):
        item = lax.rem(local, 2)
        slot = item if which == 0 else 1 + item

        @pl.when(major_home)
        def _():
            pltpu.make_async_copy(
                ins[which].at[3 * me_group + side],
                place(which, slot, me_seq),
                in_recv.at[which, item],
            ).start()

        @pl.when(jnp.logical_not(major_home))
        def _():
            major_block(which, 0, side).start()

        major_block(which, 0, 1 - side).start()

        @pl.loop(1, 16)
        def _(step):
            major_block(which, step, side).start()
            major_block(which, step, 1 - side).start()

    def start_shared(which):
        @pl.when(shared_home)
        def _():
            pltpu.make_async_copy(
                ins[which].at[3 * me_group + 2],
                place(which, item_slot(which, 2), me_seq),
                in_recv.at[which, 2],
            ).start()

        @pl.when(jnp.logical_not(shared_home))
        def _():
            shared_block(which, 0).start()

        @pl.loop(1, 16)
        def _(step):
            shared_block(which, step).start()

    def wait_item(which, item):
        ref = slot_ref(which, item_slot(which, item))
        pltpu.make_async_copy(ref, ref, in_recv.at[which, item]).wait()

    next_row = lax.rem(row + 1, 4)
    fwd_span = jnp.where(core == 0, me_span + 1, next_row * 4 + plane * 2)
    shared_row = jnp.where(side == 0, row, next_row)
    fwd_shared_span = jnp.where(core == 0, me_span + 1, shared_row * 4 + plane * 2)
    fwd_shared_seq = jnp.where(core == 0, me_seq, jnp.where(side == 0, me_seq + 1, me_seq - 1))
    last_row = row == 3
    fwd_major_sends = jnp.logical_not(jnp.logical_and(core == 1, last_row))
    fwd_shared_sends = jnp.logical_not(
        jnp.logical_and(jnp.logical_and(core == 1, side == 1), last_row)
    )
    first_row = jnp.logical_and(core == 0, row == 0)
    major_first = first_row
    shared_first = jnp.logical_and(first_row, side == 0)

    def forward(which, shared):
        return pltpu.make_async_remote_copy(
            src_ref=slot_ref(which, 4 if shared else 2),
            dst_ref=slot_ref(which, 3 if shared else 0),
            send_sem=fwd_send.at[which - 1, shared], recv_sem=fwd_recv.at[which - 1, shared],
            device_id=(fwd_shared_span, fwd_shared_seq) if shared else (fwd_span, me_seq),
            device_id_type=MESH,
        )

    def vis_block(offset):
        return pltpu.make_async_remote_copy(
            src_ref=vis_in, dst_ref=vis.at[local],
            send_sem=vis_send, recv_sem=vis_recv,
            device_id=(row * 4 + lax.rem(local + offset, 4), me_seq), device_id_type=MESH,
        )

    for offset in range(1, 4):
        vis_block(offset).start()
    pltpu.make_async_copy(vis_in, vis.at[local], vis_recv).start()
    for which in (1, 2, 0):
        start_shared(which)

    @pl.when(major_first)
    def _():
        kb[:TOKENS, :] = jnp.zeros((TOKENS, WIDTH), jnp.bfloat16)
        vb[:, :TOKENS] = jnp.zeros((WIDTH, TOKENS), jnp.bfloat16)

    @pl.when(shared_first)
    def _():
        kb[3 * TOKENS:4 * TOKENS, :] = jnp.zeros((TOKENS, WIDTH), jnp.bfloat16)
        vb[:, 3 * TOKENS:4 * TOKENS] = jnp.zeros((WIDTH, TOKENS), jnp.bfloat16)

    pltpu.make_async_copy(vis, vis, vis_recv).wait()
    tile_of = lax.broadcasted_iota(jnp.int32, (TILE, TOKENS), 1) // TILE
    pick = (tile_of == lax.broadcasted_iota(jnp.int32, (TILE, TOKENS), 0)).astype(jnp.bfloat16)
    for item in range(PER):
        seen = matmul(vis[item_spans[item]].astype(jnp.bfloat16), pick, CONTRACT_PLAIN)
        bias[item] = (1.0 - seen) * HIDDEN

    def attend(item):
        origin = base[item] * TOKENS

        @pl.loop(0, TOKENS // QB)
        def _(block):
            start = pl.multiple_of(block * QB, QB)
            columns = pl.ds(start, QB)
            query = qb[pl.ds(pl.multiple_of(item * TOKENS + start, QB), QB), :]
            chunks = TOKENS // KB + (block * QB + QB + KB - 1) // KB

            def score(chunk, largest):
                first = pl.multiple_of(chunk * KB, KB)
                part = matmul(kb[pl.ds(origin + first, KB), :], query, CONTRACT_LAST)
                scores[pl.ds(first, KB), :] = part
                for tile in range(KB // TILE):
                    rows = part[tile * TILE:(tile + 1) * TILE].reshape(TILE // 8, 8, QB)
                    hidden = bias[item, pl.ds(chunk * (KB // TILE) + tile, 1), columns]
                    largest = jnp.maximum(largest, jnp.max(rows, axis=0) + hidden)
                return largest

            largest = lax.fori_loop(0, chunks, score, jnp.full((8, QB), -3e38, jnp.float32))
            top = jnp.max(largest, axis=0, keepdims=True) * SCALE

            def weigh(chunk, carry):
                total, summed = carry
                first = pl.multiple_of(chunk * KB, KB)
                parts = []
                for tile in range(KB // TILE):
                    hidden = bias[item, pl.ds(chunk * (KB // TILE) + tile, 1), columns]
                    rows = scores[pl.ds(first + tile * TILE, TILE), :]
                    weight = jnp.exp2(rows * SCALE - (top - hidden))
                    summed = summed + jnp.sum(weight.reshape(TILE // 8, 8, QB), axis=0)
                    parts.append(weight.astype(jnp.bfloat16))
                weights = jnp.concatenate(parts, 0)
                total = total + matmul(vb[:, pl.ds(origin + first, KB)], weights, CONTRACT_PLAIN)
                return total, summed

            total, summed = lax.fori_loop(
                0, chunks, weigh,
                (jnp.zeros((WIDTH, QB), jnp.float32), jnp.zeros((8, QB), jnp.float32)),
            )
            result = total / jnp.sum(summed, axis=0, keepdims=True)
            ob[item, columns, :] = jnp.transpose(result).astype(jnp.bfloat16)

            for part in range(QB // TILE):
                tile = block * (QB // TILE) + part
                source = ob.at[item, pl.ds(pl.multiple_of(tile * TILE, TILE), TILE), :]
                here = jnp.logical_and(item_spans[item] == local, tile == me_seq)

                @pl.when(here)
                def _():
                    pltpu.make_async_copy(source, o_out.at[item_heads[item]], o_recv).start()

                @pl.when(jnp.logical_not(here))
                def _():
                    pltpu.make_async_remote_copy(
                        src_ref=source, dst_ref=o_out.at[item_heads[item]],
                        send_sem=o_send.at[item], recv_sem=o_recv,
                        device_id=(row * 4 + item_spans[item], tile), device_id_type=MESH,
                    ).start()

    for which in (1, 2):
        wait_item(which, 2)

        @pl.when(fwd_shared_sends)
        def _():
            forward(which, 1).start()

    start_major(1)
    start_major(2)
    wait_item(0, 2)

    @pl.when(jnp.logical_not(shared_first))
    def _():
        for which in (1, 2):
            ref = slot_ref(which, 3)
            pltpu.make_async_copy(ref, ref, fwd_recv.at[which - 1, 1]).wait()

    attend(2)

    for which in (1, 2):
        wait_item(which, 1)

        @pl.when(fwd_major_sends)
        def _():
            forward(which, 0).start()

    start_major(0)
    for which in (1, 2, 0):
        wait_item(which, 0)

    @pl.when(jnp.logical_not(major_first))
    def _():
        for which in (1, 2):
            ref = slot_ref(which, 0)
            pltpu.make_async_copy(ref, ref, fwd_recv.at[which - 1, 0]).wait()

    attend(0)
    wait_item(0, 1)
    attend(1)

    pltpu.make_async_copy(o_out, o_out, o_recv).wait()

    for offset in range(1, 4):
        vis_block(offset).wait_send()
    for which in (0, 1, 2):
        sent = ins[which].at[:31]
        pltpu.make_async_copy(sent, sent, in_send.at[which, 0]).wait()
        sent = ins[which].at[:15]
        pltpu.make_async_copy(sent, sent, in_send.at[which, 1]).wait()

        @pl.when(jnp.logical_not(major_home))
        def _():
            major_block(which, 0, side).wait_send()

        @pl.when(jnp.logical_not(shared_home))
        def _():
            shared_block(which, 0).wait_send()

    @pl.when(fwd_major_sends)
    def _():
        for which in (1, 2):
            forward(which, 0).wait_send()

    @pl.when(fwd_shared_sends)
    def _():
        for which in (1, 2):
            forward(which, 1).wait_send()

    for item in range(PER):
        sent = o_out.at[:15]
        pltpu.make_async_copy(sent, sent, o_send.at[item]).wait()

        @pl.when(item_spans[item] != local)
        def _():
            last = o_out.at[0]
            pltpu.make_async_copy(last, last, o_send.at[item]).wait()


def exchange_and_attend(query, keys, values, visible):
    anywhere = pl.BlockSpec(memory_space=pl.ANY)
    return pl.pallas_call(
        kernel,
        out_shape=jax.ShapeDtypeStruct((HEADS, TILE, WIDTH), jnp.bfloat16),
        in_specs=[anywhere] * 4,
        out_specs=anywhere,
        scratch_shapes=[
            pltpu.VMEM((PER * TOKENS, WIDTH), jnp.bfloat16),
            pltpu.VMEM((5 * TOKENS, WIDTH), jnp.bfloat16),
            pltpu.VMEM((WIDTH, 5 * TOKENS), jnp.bfloat16),
            pltpu.VMEM((PER, TOKENS, WIDTH), jnp.bfloat16),
            pltpu.VMEM((4, 2 * TILES, TILE), jnp.float32),
            pltpu.VMEM((PER, 2 * TILES, TOKENS), jnp.float32),
            pltpu.VMEM((2 * TOKENS, QB), jnp.float32),
            pltpu.SemaphoreType.DMA((3, 2)),
            pltpu.SemaphoreType.DMA((3, PER)),
            pltpu.SemaphoreType.DMA,
            pltpu.SemaphoreType.DMA,
            pltpu.SemaphoreType.DMA((2, 2)),
            pltpu.SemaphoreType.DMA((2, 2)),
            pltpu.SemaphoreType.DMA((PER,)),
            pltpu.SemaphoreType.DMA,
        ],
        compiler_params=pltpu.CompilerParams(
            vmem_limit_bytes=56 << 20, has_side_effects=True
        ),
        name="exchange_and_attend",
    )(query, keys, values, visible)


def visible_tiles(tile_lists, tile_counts):
    slots = jnp.arange(2 * TILES, dtype=jnp.int32)
    used = slots[None, :] < tile_counts[:, None]
    named = (tile_lists[:, :, None] == slots[None, None, :]) & used[:, :, None]
    return jnp.any(named, axis=1).T.astype(jnp.float32)


def per_device(query, keys, values, block_list, block_count):
    visible = jnp.pad(
        visible_tiles(block_list[0], block_count[0]), ((0, 0), (0, TILE - TILES))
    )
    result = exchange_and_attend(
        jnp.transpose(query[0], (1, 0, 2)),
        jnp.transpose(keys[0], (1, 0, 2)),
        jnp.transpose(values[0], (1, 2, 0)),
        visible,
    )
    return jnp.transpose(result, (1, 0, 2))[None]


def solution(mesh):
    in_specs = (
        P("span", "seq", None, None),
        P("span", "seq", None, None),
        P("span", "seq", None, None),
        P("span", None, None),
        P("span", None),
    )
    out_specs = P("span", "seq", None, None)
    return jax.shard_map(
        per_device, mesh=mesh, in_specs=in_specs, out_specs=out_specs, check_vma=False
    )
```

```python
import functools
import math

import jax
import jax.numpy as jnp
from jax import lax
from jax.experimental import pallas as pl
from jax.experimental.pallas import tpu as pltpu
from jax.sharding import PartitionSpec as P

MESH = pl.DeviceIdType.MESH
TILE = 128
TILES = 16
TOKENS = TILE * TILES
SPANS = 16
SEQ = 16
HEADS = 48
PER = HEADS // SEQ
WIDTH = 128
QB = 512
KB = 1024
SCALE = math.log2(math.e) / math.sqrt(WIDTH)
HIDDEN = -1e30
CONTRACT_LAST = (((1,), (1,)), ((), ()))
CONTRACT_FIRST = (((0,), (0,)), ((), ()))
CONTRACT_PLAIN = (((1,), (0,)), ((), ()))


def matmul(left, right, dims):
    return lax.dot_general(left, right, dims, preferred_element_type=jnp.float32)


def kernel(
    q_raw, k_raw, v_raw, list_in, count_in, o_out,
    loaded, ins, arrived, vis_in, qb, kb, vb, ob, vis, bias, scores, load,
    in_send, in_recv, vis_send, vis_recv, fwd_send, fwd_recv, o_send, o_recv,
):
    me_span = lax.axis_index("span")
    me_seq = lax.axis_index("seq")
    row = me_span // 4
    local = lax.rem(me_span, 4)
    core = lax.rem(me_span, 2)
    plane = lax.rem(me_span // 2, 2)
    x = lax.rem(me_seq, 4)
    side = lax.rem(x, 2)
    z = me_seq // 4 * 2 + plane
    me_group = x // 2 * 8 + z
    item_spans = (2 * core, 2 * core + 1, 2 * side + core)
    item_heads = (3 * me_group + side, 3 * me_group + side, 3 * me_group + 2)

    base = (0, 1, 3)

    def place(which, slot, tile):
        at = pl.ds(pl.multiple_of(slot * TOKENS + tile * TILE, TILE), TILE)
        if which == 0:
            return qb.at[at, :]
        if which == 1:
            return kb.at[at, :]
        return vb.at[:, at]

    def slot_ref(which, slot):
        at = pl.ds(slot * TOKENS, TOKENS)
        if which == 0:
            return qb.at[at, :]
        if which == 1:
            return kb.at[at, :]
        return vb.at[:, at]

    def item_slot(which, item):
        return item if which == 0 else base[item] + 1

    def chip(group, x_side, its_core):
        its_z = lax.rem(group, 8)
        return (
            row * 4 + lax.rem(its_z, 2) * 2 + its_core,
            its_z // 2 * 4 + group // 8 * 2 + x_side,
        )

    def major_block(which, step, x_side):
        group = lax.rem(me_group + step, 16)
        item = lax.rem(local, 2)
        slot = item if which == 0 else 1 + item
        return pltpu.make_async_remote_copy(
            src_ref=ins.at[which, 3 * group + x_side],
            dst_ref=place(which, slot, me_seq),
            send_sem=in_send.at[which, 0], recv_sem=in_recv.at[which, item],
            device_id=chip(group, x_side, local // 2), device_id_type=MESH,
        )

    def shared_block(which, step):
        group = lax.rem(me_group + step, 16)
        return pltpu.make_async_remote_copy(
            src_ref=ins.at[which, 3 * group + 2],
            dst_ref=place(which, item_slot(which, 2), me_seq),
            send_sem=in_send.at[which, 1], recv_sem=in_recv.at[which, 2],
            device_id=chip(group, local // 2, lax.rem(local, 2)), device_id_type=MESH,
        )

    major_home = local // 2 == core
    shared_home = local // 2 == side

    def start_major(which):
        item = lax.rem(local, 2)
        slot = item if which == 0 else 1 + item

        @pl.when(major_home)
        def _():
            pltpu.make_async_copy(
                ins.at[which, 3 * me_group + side],
                place(which, slot, me_seq),
                in_recv.at[which, item],
            ).start()

        @pl.when(jnp.logical_not(major_home))
        def _():
            major_block(which, 0, side).start()

        major_block(which, 0, 1 - side).start()

        @pl.loop(1, 16)
        def _(step):
            major_block(which, step, side).start()
            major_block(which, step, 1 - side).start()

    def start_shared(which):
        @pl.when(shared_home)
        def _():
            pltpu.make_async_copy(
                ins.at[which, 3 * me_group + 2],
                place(which, item_slot(which, 2), me_seq),
                in_recv.at[which, 2],
            ).start()

        @pl.when(jnp.logical_not(shared_home))
        def _():
            shared_block(which, 0).start()

        @pl.loop(1, 16)
        def _(step):
            shared_block(which, step).start()

    def wait_item(which, item):
        ref = slot_ref(which, item_slot(which, item))
        pltpu.make_async_copy(ref, ref, in_recv.at[which, item]).wait()

    next_row = lax.rem(row + 1, 4)
    fwd_span = jnp.where(core == 0, me_span + 1, next_row * 4 + plane * 2)
    shared_row = jnp.where(side == 0, row, next_row)
    fwd_shared_span = jnp.where(core == 0, me_span + 1, shared_row * 4 + plane * 2)
    fwd_shared_seq = jnp.where(core == 0, me_seq, jnp.where(side == 0, me_seq + 1, me_seq - 1))
    last_row = row == 3
    fwd_major_sends = jnp.logical_not(jnp.logical_and(core == 1, last_row))
    fwd_shared_sends = jnp.logical_not(
        jnp.logical_and(jnp.logical_and(core == 1, side == 1), last_row)
    )
    first_row = jnp.logical_and(core == 0, row == 0)
    major_first = first_row
    shared_first = jnp.logical_and(first_row, side == 0)

    def forward(which, shared):
        return pltpu.make_async_remote_copy(
            src_ref=slot_ref(which, 4 if shared else 2),
            dst_ref=slot_ref(which, 3 if shared else 0),
            send_sem=fwd_send.at[which - 1, shared], recv_sem=fwd_recv.at[which - 1, shared],
            device_id=(fwd_shared_span, fwd_shared_seq) if shared else (fwd_span, me_seq),
            device_id_type=MESH,
        )

    def vis_block(offset):
        return pltpu.make_async_remote_copy(
            src_ref=vis_in, dst_ref=vis.at[local],
            send_sem=vis_send, recv_sem=vis_recv,
            device_id=(row * 4 + lax.rem(local + offset, 4), me_seq), device_id_type=MESH,
        )

    loads = [
        pltpu.make_async_copy(raw, loaded.at[which], load.at[which])
        for which, raw in enumerate((q_raw, k_raw, v_raw))
    ]
    for which in (1, 2, 0):
        loads[which].start()

    barrier = pltpu.get_barrier_semaphore()

    @pl.loop(1, 64)
    def _(step):
        other = lax.rem(local * 16 + me_seq + step, 64)
        pl.semaphore_signal(
            barrier, inc=1, device_id=(row * 4 + other // 16, lax.rem(other, 16)),
            device_id_type=MESH,
        )

    row_before = lax.rem(row + 3, 4) * 4 + plane * 2 + 1

    @pl.when(core == 0)
    def _():
        pl.semaphore_signal(
            barrier, inc=1, device_id=(row_before, me_seq), device_id_type=MESH
        )

    @pl.when(jnp.logical_and(core == 0, side == 0))
    def _():
        pl.semaphore_signal(
            barrier, inc=1, device_id=(row_before, me_seq + 1), device_id_type=MESH
        )

    column = lax.broadcasted_iota(jnp.int32, (TILES, TILE), 1)
    diagonal = lax.broadcasted_iota(jnp.int32, (TILES, TILES), 0) == lax.broadcasted_iota(
        jnp.int32, (TILES, TILES), 1
    )
    count = jnp.sum(
        jnp.where(diagonal, count_in[...].astype(jnp.float32), 0.0), axis=1, keepdims=True
    )
    seen = jnp.zeros((TILES, TILE), jnp.float32)
    for slot in range(2 * TILES):
        named = jnp.logical_and(list_in[:, slot:slot + 1] == column, count > slot)
        seen = jnp.where(named, 1.0, seen)
    vis_in[...] = seen

    for which in (1, 2, 0):
        loads[which].wait()
        ins[which] = jnp.transpose(loaded[which], (1, 0, 2))
        if which == 2:
            @pl.loop(0, HEADS // 4)
            def _(four):
                for part in range(4):
                    ins[2, 4 * four + part] = jnp.transpose(ins[2, 4 * four + part])

    pl.semaphore_wait(barrier, 63 + core * (1 + side))

    for offset in range(1, 4):
        vis_block(offset).start()
    pltpu.make_async_copy(vis_in, vis.at[local], vis_recv).start()
    for which in (1, 2):
        start_shared(which)
    start_major(1)

    @pl.when(major_first)
    def _():
        kb[:TOKENS, :] = jnp.zeros((TOKENS, WIDTH), jnp.bfloat16)
        vb[:, :TOKENS] = jnp.zeros((WIDTH, TOKENS), jnp.bfloat16)

    @pl.when(shared_first)
    def _():
        kb[3 * TOKENS:4 * TOKENS, :] = jnp.zeros((TOKENS, WIDTH), jnp.bfloat16)
        vb[:, 3 * TOKENS:4 * TOKENS] = jnp.zeros((WIDTH, TOKENS), jnp.bfloat16)

    pltpu.make_async_copy(vis, vis, vis_recv).wait()
    tile_of = lax.broadcasted_iota(jnp.int32, (TILES, TOKENS), 1) // TILE
    pick = (tile_of == lax.broadcasted_iota(jnp.int32, (TILES, TOKENS), 0)).astype(jnp.bfloat16)
    for item in range(PER):
        seen = matmul(vis[item_spans[item]].astype(jnp.bfloat16), pick, CONTRACT_FIRST)
        bias[item] = (1.0 - seen[:2 * TILES]) * HIDDEN

    def attend(item):
        origin = base[item] * TOKENS

        @pl.loop(0, TOKENS // QB)
        def _(block):
            start = pl.multiple_of(block * QB, QB)
            columns = pl.ds(start, QB)
            query = qb[pl.ds(pl.multiple_of(item * TOKENS + start, QB), QB), :]
            chunks = TOKENS // KB + (block * QB + QB + KB - 1) // KB

            def score(chunk, largest):
                first = pl.multiple_of(chunk * KB, KB)
                part = matmul(kb[pl.ds(origin + first, KB), :], query, CONTRACT_LAST)
                scores[pl.ds(first, KB), :] = part
                for tile in range(KB // TILE):
                    rows = part[tile * TILE:(tile + 1) * TILE].reshape(TILE // 8, 8, QB)
                    hidden = bias[item, pl.ds(chunk * (KB // TILE) + tile, 1), columns]
                    largest = jnp.maximum(largest, jnp.max(rows, axis=0) + hidden)
                return largest

            largest = lax.fori_loop(0, chunks, score, jnp.full((8, QB), -3e38, jnp.float32))
            top = jnp.max(largest, axis=0, keepdims=True) * SCALE

            def weigh(chunk, carry):
                total, summed = carry
                first = pl.multiple_of(chunk * KB, KB)
                parts = []
                for tile in range(KB // TILE):
                    hidden = bias[item, pl.ds(chunk * (KB // TILE) + tile, 1), columns]
                    rows = scores[pl.ds(first + tile * TILE, TILE), :]
                    weight = jnp.exp2(rows * SCALE - (top - hidden))
                    summed = summed + jnp.sum(weight.reshape(TILE // 8, 8, QB), axis=0)
                    parts.append(weight.astype(jnp.bfloat16))
                weights = jnp.concatenate(parts, 0)
                total = total + matmul(vb[:, pl.ds(origin + first, KB)], weights, CONTRACT_PLAIN)
                return total, summed

            total, summed = lax.fori_loop(
                0, chunks, weigh,
                (jnp.zeros((WIDTH, QB), jnp.float32), jnp.zeros((8, QB), jnp.float32)),
            )
            result = total / jnp.sum(summed, axis=0, keepdims=True)
            ob[item, columns, :] = jnp.transpose(result).astype(jnp.bfloat16)

            for part in range(QB // TILE):
                tile = block * (QB // TILE) + part
                source = ob.at[item, pl.ds(pl.multiple_of(tile * TILE, TILE), TILE), :]
                here = jnp.logical_and(item_spans[item] == local, tile == me_seq)

                @pl.when(here)
                def _():
                    pltpu.make_async_copy(source, arrived.at[item_heads[item]], o_recv).start()

                @pl.when(jnp.logical_not(here))
                def _():
                    pltpu.make_async_remote_copy(
                        src_ref=source, dst_ref=arrived.at[item_heads[item]],
                        send_sem=o_send.at[item], recv_sem=o_recv,
                        device_id=(row * 4 + item_spans[item], tile), device_id_type=MESH,
                    ).start()

    for which in (1, 2):
        wait_item(which, 2)

        @pl.when(fwd_shared_sends)
        def _():
            forward(which, 1).start()

    start_major(2)

    wait_item(1, 1)

    @pl.when(fwd_major_sends)
    def _():
        forward(1, 0).start()

    start_major(0)
    wait_item(2, 1)

    @pl.when(fwd_major_sends)
    def _():
        forward(2, 0).start()

    start_shared(0)
    for which in (1, 2, 0):
        wait_item(which, 0)

    @pl.when(jnp.logical_not(major_first))
    def _():
        for which in (1, 2):
            ref = slot_ref(which, 0)
            pltpu.make_async_copy(ref, ref, fwd_recv.at[which - 1, 0]).wait()

    attend(0)
    wait_item(0, 1)
    attend(1)
    wait_item(0, 2)

    @pl.when(jnp.logical_not(shared_first))
    def _():
        for which in (1, 2):
            ref = slot_ref(which, 3)
            pltpu.make_async_copy(ref, ref, fwd_recv.at[which - 1, 1]).wait()

    attend(2)

    pltpu.make_async_copy(arrived, arrived, o_recv).wait()
    o_out[...] = jnp.transpose(arrived[...], (1, 0, 2))

    for offset in range(1, 4):
        vis_block(offset).wait_send()
    for which in (0, 1, 2):
        sent = ins.at[which, :31]
        pltpu.make_async_copy(sent, sent, in_send.at[which, 0]).wait()
        sent = ins.at[which, :15]
        pltpu.make_async_copy(sent, sent, in_send.at[which, 1]).wait()

        @pl.when(jnp.logical_not(major_home))
        def _():
            major_block(which, 0, side).wait_send()

        @pl.when(jnp.logical_not(shared_home))
        def _():
            shared_block(which, 0).wait_send()

    @pl.when(fwd_major_sends)
    def _():
        for which in (1, 2):
            forward(which, 0).wait_send()

    @pl.when(fwd_shared_sends)
    def _():
        for which in (1, 2):
            forward(which, 1).wait_send()

    for item in range(PER):
        sent = arrived.at[:15]
        pltpu.make_async_copy(sent, sent, o_send.at[item]).wait()

        @pl.when(item_spans[item] != local)
        def _():
            last = arrived.at[0]
            pltpu.make_async_copy(last, last, o_send.at[item]).wait()


def per_device(query, keys, values, block_list, block_count):
    anywhere = pl.BlockSpec(memory_space=pl.ANY)
    vmem = pl.BlockSpec(memory_space=pltpu.VMEM)
    return pl.pallas_call(
        kernel,
        out_shape=jax.ShapeDtypeStruct((TILE, HEADS, WIDTH), jnp.bfloat16),
        in_specs=[anywhere, anywhere, anywhere, vmem, vmem],
        out_specs=vmem,
        scratch_shapes=[
            pltpu.VMEM((3, TILE, HEADS, WIDTH), jnp.bfloat16),
            pltpu.VMEM((3, HEADS, TILE, WIDTH), jnp.bfloat16),
            pltpu.VMEM((HEADS, TILE, WIDTH), jnp.bfloat16),
            pltpu.VMEM((TILES, TILE), jnp.float32),
            pltpu.VMEM((PER * TOKENS, WIDTH), jnp.bfloat16),
            pltpu.VMEM((5 * TOKENS, WIDTH), jnp.bfloat16),
            pltpu.VMEM((WIDTH, 5 * TOKENS), jnp.bfloat16),
            pltpu.VMEM((PER, TOKENS, WIDTH), jnp.bfloat16),
            pltpu.VMEM((4, TILES, TILE), jnp.float32),
            pltpu.VMEM((PER, 2 * TILES, TOKENS), jnp.float32),
            pltpu.VMEM((2 * TOKENS, QB), jnp.float32),
            pltpu.SemaphoreType.DMA((3,)),
            pltpu.SemaphoreType.DMA((3, 2)),
            pltpu.SemaphoreType.DMA((3, PER)),
            pltpu.SemaphoreType.DMA,
            pltpu.SemaphoreType.DMA,
            pltpu.SemaphoreType.DMA((2, 2)),
            pltpu.SemaphoreType.DMA((2, 2)),
            pltpu.SemaphoreType.DMA((PER,)),
            pltpu.SemaphoreType.DMA,
        ],
        compiler_params=pltpu.CompilerParams(
            vmem_limit_bytes=56 << 20, has_side_effects=True, collective_id=0
        ),
        name="exchange_and_attend",
    )(query[0], keys[0], values[0], block_list[0], block_count)[None]


def solution(mesh):
    in_specs = (
        P("span", "seq", None, None),
        P("span", "seq", None, None),
        P("span", "seq", None, None),
        P("span", None, None),
        P("span", None),
    )
    out_specs = P("span", "seq", None, None)
    return jax.shard_map(
        per_device, mesh=mesh, in_specs=in_specs, out_specs=out_specs, check_vma=False
    )
```

```python
import functools
import math

import jax
import jax.numpy as jnp
from jax import lax
from jax.experimental import pallas as pl
from jax.experimental.pallas import tpu as pltpu
from jax.sharding import PartitionSpec as P

MESH = pl.DeviceIdType.MESH
TILE = 128
TILES = 16
TOKENS = TILE * TILES
SPANS = 16
SEQ = 16
HEADS = 48
PER = HEADS // SEQ
WIDTH = 128
QB = 256
KB = 256
SCALE = math.log2(math.e) / math.sqrt(WIDTH)
HIDDEN = -1e30
CONTRACT_LAST = (((1,), (1,)), ((), ()))
CONTRACT_FIRST = (((0,), (0,)), ((), ()))
CONTRACT_PLAIN = (((1,), (0,)), ((), ()))


def matmul(left, right, dims):
    return lax.dot_general(left, right, dims, preferred_element_type=jnp.float32)


def kernel(
    q_raw, k_raw, v_raw, list_in, count_in, o_out,
    loaded, ins, arrived, vis_in, qb, kb, vb, ob, vis, bias, scores, load,
    in_send, in_recv, vis_send, vis_recv, fwd_send, fwd_recv, o_send, o_recv,
):
    me_span = lax.axis_index("span")
    me_seq = lax.axis_index("seq")
    row = me_span // 4
    local = lax.rem(me_span, 4)
    core = lax.rem(me_span, 2)
    plane = lax.rem(me_span // 2, 2)
    x = lax.rem(me_seq, 4)
    side = lax.rem(x, 2)
    z = me_seq // 4 * 2 + plane
    me_group = x // 2 * 8 + z
    item_spans = (2 * core, 2 * core + 1, 2 * side + core)

    base = (0, 1, 3)

    def place(which, slot, tile):
        at = pl.ds(pl.multiple_of(slot * TOKENS + tile * TILE, TILE), TILE)
        if which == 0:
            return qb.at[at, :]
        if which == 1:
            return kb.at[at, :]
        return vb.at[:, at]

    def slot_ref(which, slot):
        at = pl.ds(slot * TOKENS, TOKENS)
        if which == 0:
            return qb.at[at, :]
        if which == 1:
            return kb.at[at, :]
        return vb.at[:, at]

    def item_slot(which, item):
        return item if which == 0 else base[item] + 1

    def chip(group, x_side, its_core):
        its_z = lax.rem(group, 8)
        return (
            row * 4 + lax.rem(its_z, 2) * 2 + its_core,
            its_z // 2 * 4 + group // 8 * 2 + x_side,
        )

    def major_block(which, step, x_side):
        group = lax.rem(me_group + step, 16)
        item = lax.rem(local, 2)
        slot = item if which == 0 else 1 + item
        return pltpu.make_async_remote_copy(
            src_ref=ins.at[which, 3 * group + x_side],
            dst_ref=place(which, slot, me_seq),
            send_sem=in_send.at[which, 0], recv_sem=in_recv.at[which, item],
            device_id=chip(group, x_side, local // 2), device_id_type=MESH,
        )

    def shared_block(which, step):
        group = lax.rem(me_group + step, 16)
        return pltpu.make_async_remote_copy(
            src_ref=ins.at[which, 3 * group + 2],
            dst_ref=place(which, item_slot(which, 2), me_seq),
            send_sem=in_send.at[which, 1], recv_sem=in_recv.at[which, 2],
            device_id=chip(group, local // 2, lax.rem(local, 2)), device_id_type=MESH,
        )

    major_home = local // 2 == core
    shared_home = local // 2 == side

    def start_major(which):
        item = lax.rem(local, 2)
        slot = item if which == 0 else 1 + item

        @pl.when(major_home)
        def _():
            pltpu.make_async_copy(
                ins.at[which, 3 * me_group + side],
                place(which, slot, me_seq),
                in_recv.at[which, item],
            ).start()

        @pl.when(jnp.logical_not(major_home))
        def _():
            major_block(which, 0, side).start()

        major_block(which, 0, 1 - side).start()

        @pl.loop(1, 16)
        def _(step):
            major_block(which, step, side).start()
            major_block(which, step, 1 - side).start()

    def start_shared(which):
        @pl.when(shared_home)
        def _():
            pltpu.make_async_copy(
                ins.at[which, 3 * me_group + 2],
                place(which, item_slot(which, 2), me_seq),
                in_recv.at[which, 2],
            ).start()

        @pl.when(jnp.logical_not(shared_home))
        def _():
            shared_block(which, 0).start()

        @pl.loop(1, 16)
        def _(step):
            shared_block(which, step).start()

    def wait_item(which, item):
        ref = slot_ref(which, item_slot(which, item))
        pltpu.make_async_copy(ref, ref, in_recv.at[which, item]).wait()

    next_row = lax.rem(row + 1, 4)
    fwd_span = jnp.where(core == 0, me_span + 1, next_row * 4 + plane * 2)
    shared_row = jnp.where(side == 0, row, next_row)
    fwd_shared_span = jnp.where(core == 0, me_span + 1, shared_row * 4 + plane * 2)
    fwd_shared_seq = jnp.where(core == 0, me_seq, jnp.where(side == 0, me_seq + 1, me_seq - 1))
    last_row = row == 3
    fwd_major_sends = jnp.logical_not(jnp.logical_and(core == 1, last_row))
    fwd_shared_sends = jnp.logical_not(
        jnp.logical_and(jnp.logical_and(core == 1, side == 1), last_row)
    )
    first_row = jnp.logical_and(core == 0, row == 0)
    major_first = first_row
    shared_first = jnp.logical_and(first_row, side == 0)

    def forward(which, shared):
        return pltpu.make_async_remote_copy(
            src_ref=slot_ref(which, 4 if shared else 2),
            dst_ref=slot_ref(which, 3 if shared else 0),
            send_sem=fwd_send.at[which - 1, shared], recv_sem=fwd_recv.at[which - 1, shared],
            device_id=(fwd_shared_span, fwd_shared_seq) if shared else (fwd_span, me_seq),
            device_id_type=MESH,
        )

    def vis_block(offset):
        return pltpu.make_async_remote_copy(
            src_ref=vis_in, dst_ref=vis.at[local],
            send_sem=vis_send, recv_sem=vis_recv,
            device_id=(row * 4 + lax.rem(local + offset, 4), me_seq), device_id_type=MESH,
        )

    loads = [
        pltpu.make_async_copy(raw, loaded.at[which], load.at[which])
        for which, raw in enumerate((q_raw, k_raw, v_raw))
    ]
    for which in (1, 2, 0):
        loads[which].start()

    barrier = pltpu.get_barrier_semaphore()

    @pl.loop(1, 64)
    def _(step):
        other = lax.rem(local * 16 + me_seq + step, 64)
        pl.semaphore_signal(
            barrier, inc=1, device_id=(row * 4 + other // 16, lax.rem(other, 16)),
            device_id_type=MESH,
        )

    row_before = lax.rem(row + 3, 4) * 4 + plane * 2 + 1

    @pl.when(core == 0)
    def _():
        pl.semaphore_signal(
            barrier, inc=1, device_id=(row_before, me_seq), device_id_type=MESH
        )

    @pl.when(jnp.logical_and(core == 0, side == 0))
    def _():
        pl.semaphore_signal(
            barrier, inc=1, device_id=(row_before, me_seq + 1), device_id_type=MESH
        )

    column = lax.broadcasted_iota(jnp.int32, (TILES, TILE), 1)
    diagonal = lax.broadcasted_iota(jnp.int32, (TILES, TILES), 0) == lax.broadcasted_iota(
        jnp.int32, (TILES, TILES), 1
    )
    count = jnp.sum(
        jnp.where(diagonal, count_in[...].astype(jnp.float32), 0.0), axis=1, keepdims=True
    )
    seen = jnp.zeros((TILES, TILE), jnp.float32)
    for slot in range(2 * TILES):
        named = jnp.logical_and(list_in[:, slot:slot + 1] == column, count > slot)
        seen = jnp.where(named, 1.0, seen)
    vis_in[...] = seen

    for which in (1, 2, 0):
        loads[which].wait()
        ins[which] = jnp.transpose(loaded[which], (1, 0, 2))
        if which == 2:
            @pl.loop(0, HEADS // 4)
            def _(four):
                for part in range(4):
                    ins[2, 4 * four + part] = jnp.transpose(ins[2, 4 * four + part])

    pl.semaphore_wait(barrier, 63 + core * (1 + side))

    for offset in range(1, 4):
        vis_block(offset).start()
    pltpu.make_async_copy(vis_in, vis.at[local], vis_recv).start()
    for which in (1, 2):
        start_shared(which)
    start_major(1)

    @pl.when(major_first)
    def _():
        kb[:TOKENS, :] = jnp.zeros((TOKENS, WIDTH), jnp.bfloat16)
        vb[:, :TOKENS] = jnp.zeros((WIDTH, TOKENS), jnp.bfloat16)

    @pl.when(shared_first)
    def _():
        kb[3 * TOKENS:4 * TOKENS, :] = jnp.zeros((TOKENS, WIDTH), jnp.bfloat16)
        vb[:, 3 * TOKENS:4 * TOKENS] = jnp.zeros((WIDTH, TOKENS), jnp.bfloat16)

    pltpu.make_async_copy(vis, vis, vis_recv).wait()
    tile_of = lax.broadcasted_iota(jnp.int32, (TILES, TOKENS), 1) // TILE
    pick = (tile_of == lax.broadcasted_iota(jnp.int32, (TILES, TOKENS), 0)).astype(jnp.bfloat16)
    for item in range(PER):
        seen = matmul(vis[item_spans[item]].astype(jnp.bfloat16), pick, CONTRACT_FIRST)
        bias[item] = (1.0 - seen[:2 * TILES]) * HIDDEN

    def attend(item):
        shared = item == 2
        origin = pl.multiple_of(jnp.where(shared, 3, item) * TOKENS, TOKENS)
        item_span = jnp.where(shared, 2 * side + core, 2 * core + item)
        item_head = 3 * me_group + jnp.where(shared, 2, side)

        def block_result(block):
            columns = slice(block * QB, (block + 1) * QB)
            query = qb[pl.ds(pl.multiple_of(item * TOKENS + block * QB, QB), QB), :]
            held = scores.at[block % 2]
            keys_seen = TOKENS + (block + 1) * QB

            def hidden(tile):
                return bias[item, tile:tile + 1, columns]

            largest = jnp.full((8, QB), -3e38, jnp.float32)
            for first in range(0, keys_seen, KB):
                part = matmul(kb[pl.ds(origin + first, KB), :], query, CONTRACT_LAST)
                held[first:first + KB, :] = part
                for at in range(0, KB, TILE):
                    rows = part[at:at + TILE].reshape(TILE // 8, 8, QB)
                    largest = jnp.maximum(
                        largest, jnp.max(rows, axis=0) + hidden((first + at) // TILE)
                    )
            top = jnp.max(largest, axis=0, keepdims=True) * SCALE

            total = jnp.zeros((WIDTH, QB), jnp.float32)
            summed = jnp.zeros((8, QB), jnp.float32)
            for first in range(0, keys_seen, KB):
                parts = []
                for at in range(first, first + KB, TILE):
                    weight = jnp.exp2(held[at:at + TILE, :] * SCALE - (top - hidden(at // TILE)))
                    summed = summed + jnp.sum(weight.reshape(TILE // 8, 8, QB), axis=0)
                    parts.append(weight.astype(jnp.bfloat16))
                weights = jnp.concatenate(parts, 0)
                total = total + matmul(
                    vb[:, pl.ds(pl.multiple_of(origin + first, KB), KB)], weights, CONTRACT_PLAIN
                )
            result = total / jnp.sum(summed, axis=0, keepdims=True)
            ob[item, columns, :] = jnp.transpose(result).astype(jnp.bfloat16)

        for block in range(TOKENS // QB):
            block_result(block)

            @pl.loop(block * (QB // TILE), (block + 1) * (QB // TILE))
            def _(tile):
                source = ob.at[item, pl.ds(pl.multiple_of(tile * TILE, TILE), TILE), :]
                here = jnp.logical_and(item_span == local, tile == me_seq)

                @pl.when(here)
                def _():
                    pltpu.make_async_copy(source, arrived.at[item_head], o_recv).start()

                @pl.when(jnp.logical_not(here))
                def _():
                    pltpu.make_async_remote_copy(
                        src_ref=source, dst_ref=arrived.at[item_head],
                        send_sem=o_send.at[item], recv_sem=o_recv,
                        device_id=(row * 4 + item_span, tile), device_id_type=MESH,
                    ).start()

    for which in (1, 2):
        wait_item(which, 2)

        @pl.when(fwd_shared_sends)
        def _():
            forward(which, 1).start()

    start_major(2)

    wait_item(1, 1)

    @pl.when(fwd_major_sends)
    def _():
        forward(1, 0).start()

    start_major(0)
    wait_item(2, 1)

    @pl.when(fwd_major_sends)
    def _():
        forward(2, 0).start()

    start_shared(0)
    for which in (1, 2, 0):
        wait_item(which, 0)

    @pl.when(jnp.logical_not(major_first))
    def _():
        for which in (1, 2):
            ref = slot_ref(which, 0)
            pltpu.make_async_copy(ref, ref, fwd_recv.at[which - 1, 0]).wait()

    wait_item(0, 1)

    @pl.loop(0, PER)
    def _(item):
        @pl.when(item == 2)
        def _():
            wait_item(0, 2)

            @pl.when(jnp.logical_not(shared_first))
            def _():
                for which in (1, 2):
                    ref = slot_ref(which, 3)
                    pltpu.make_async_copy(ref, ref, fwd_recv.at[which - 1, 1]).wait()

        attend(item)

    pltpu.make_async_copy(arrived, arrived, o_recv).wait()
    o_out[...] = jnp.transpose(arrived[...], (1, 0, 2))

    for offset in range(1, 4):
        vis_block(offset).wait_send()
    for which in (0, 1, 2):
        sent = ins.at[which, :31]
        pltpu.make_async_copy(sent, sent, in_send.at[which, 0]).wait()
        sent = ins.at[which, :15]
        pltpu.make_async_copy(sent, sent, in_send.at[which, 1]).wait()

        @pl.when(jnp.logical_not(major_home))
        def _():
            major_block(which, 0, side).wait_send()

        @pl.when(jnp.logical_not(shared_home))
        def _():
            shared_block(which, 0).wait_send()

    @pl.when(fwd_major_sends)
    def _():
        for which in (1, 2):
            forward(which, 0).wait_send()

    @pl.when(fwd_shared_sends)
    def _():
        for which in (1, 2):
            forward(which, 1).wait_send()

    for item in range(PER):
        sent = arrived.at[:15]
        pltpu.make_async_copy(sent, sent, o_send.at[item]).wait()

        @pl.when(item_spans[item] != local)
        def _():
            last = arrived.at[0]
            pltpu.make_async_copy(last, last, o_send.at[item]).wait()


def per_device(query, keys, values, block_list, block_count):
    anywhere = pl.BlockSpec(memory_space=pl.ANY)
    vmem = pl.BlockSpec(memory_space=pltpu.VMEM)
    return pl.pallas_call(
        kernel,
        out_shape=jax.ShapeDtypeStruct((TILE, HEADS, WIDTH), jnp.bfloat16),
        in_specs=[anywhere, anywhere, anywhere, vmem, vmem],
        out_specs=vmem,
        scratch_shapes=[
            pltpu.VMEM((3, TILE, HEADS, WIDTH), jnp.bfloat16),
            pltpu.VMEM((3, HEADS, TILE, WIDTH), jnp.bfloat16),
            pltpu.VMEM((HEADS, TILE, WIDTH), jnp.bfloat16),
            pltpu.VMEM((TILES, TILE), jnp.float32),
            pltpu.VMEM((PER * TOKENS, WIDTH), jnp.bfloat16),
            pltpu.VMEM((5 * TOKENS, WIDTH), jnp.bfloat16),
            pltpu.VMEM((WIDTH, 5 * TOKENS), jnp.bfloat16),
            pltpu.VMEM((PER, TOKENS, WIDTH), jnp.bfloat16),
            pltpu.VMEM((4, TILES, TILE), jnp.float32),
            pltpu.VMEM((PER, 2 * TILES, TOKENS), jnp.float32),
            pltpu.VMEM((2, 2 * TOKENS, QB), jnp.float32),
            pltpu.SemaphoreType.DMA((3,)),
            pltpu.SemaphoreType.DMA((3, 2)),
            pltpu.SemaphoreType.DMA((3, PER)),
            pltpu.SemaphoreType.DMA,
            pltpu.SemaphoreType.DMA,
            pltpu.SemaphoreType.DMA((2, 2)),
            pltpu.SemaphoreType.DMA((2, 2)),
            pltpu.SemaphoreType.DMA((PER,)),
            pltpu.SemaphoreType.DMA,
        ],
        compiler_params=pltpu.CompilerParams(
            vmem_limit_bytes=56 << 20, has_side_effects=True, collective_id=0
        ),
        name="exchange_and_attend",
    )(query[0], keys[0], values[0], block_list[0], block_count)[None]


def solution(mesh):
    in_specs = (
        P("span", "seq", None, None),
        P("span", "seq", None, None),
        P("span", "seq", None, None),
        P("span", None, None),
        P("span", None),
    )
    out_specs = P("span", "seq", None, None)
    return jax.shard_map(
        per_device, mesh=mesh, in_specs=in_specs, out_specs=out_specs, check_vma=False
    )
```

```python
import functools
import math

import jax
import jax.numpy as jnp
from jax import lax
from jax.experimental import pallas as pl
from jax.experimental.pallas import tpu as pltpu
from jax.sharding import PartitionSpec as P

MESH = pl.DeviceIdType.MESH
TILE = 128
TILES = 16
TOKENS = TILE * TILES
SPANS = 16
SEQ = 16
HEADS = 48
PER = HEADS // SEQ
WIDTH = 128
QB = 256
KB = 256
SCALE = math.log2(math.e) / math.sqrt(WIDTH)
HIDDEN = -1e30
CONTRACT_LAST = (((1,), (1,)), ((), ()))
CONTRACT_FIRST = (((0,), (0,)), ((), ()))
CONTRACT_PLAIN = (((1,), (0,)), ((), ()))


def matmul(left, right, dims):
    return lax.dot_general(left, right, dims, preferred_element_type=jnp.float32)


def kernel(
    q_raw, k_raw, v_raw, list_in, count_in, arrived,
    loaded, ins, vis_in, qb, kb, vb, ob, vis, bias, scores, load,
    in_send, in_recv, vis_send, vis_recv, fwd_send, fwd_recv, o_send, o_recv,
):
    me_span = lax.axis_index("span")
    me_seq = lax.axis_index("seq")
    row = me_span // 4
    local = lax.rem(me_span, 4)
    core = lax.rem(me_span, 2)
    plane = lax.rem(me_span // 2, 2)
    x = lax.rem(me_seq, 4)
    side = lax.rem(x, 2)
    z = me_seq // 4 * 2 + plane
    me_group = x // 2 * 8 + z
    item_spans = (2 * core, 2 * core + 1, 2 * side + core)

    base = (0, 1, 3)

    def place(which, slot, tile):
        at = pl.ds(pl.multiple_of(slot * TOKENS + tile * TILE, TILE), TILE)
        if which == 0:
            return qb.at[at, :]
        if which == 1:
            return kb.at[at, :]
        return vb.at[:, at]

    def slot_ref(which, slot):
        at = pl.ds(slot * TOKENS, TOKENS)
        if which == 0:
            return qb.at[at, :]
        if which == 1:
            return kb.at[at, :]
        return vb.at[:, at]

    def item_slot(which, item):
        return item if which == 0 else base[item] + 1

    def group_at(step):
        turn = step // 2
        far = (turn + 1) // 2
        z_step = (lax.rem(turn, 2) * 2 * far - far) * (1 - 2 * side)
        return lax.rem(x // 2 + step, 2) * 8 + lax.rem(z + z_step + 8, 8)

    def chip(group, x_side, its_core):
        its_z = lax.rem(group, 8)
        return (
            row * 4 + lax.rem(its_z, 2) * 2 + its_core,
            its_z // 2 * 4 + group // 8 * 2 + x_side,
        )

    def major_block(which, step, x_side):
        group = group_at(step)
        item = lax.rem(local, 2)
        slot = item if which == 0 else 1 + item
        return pltpu.make_async_remote_copy(
            src_ref=ins.at[which, 3 * group + x_side],
            dst_ref=place(which, slot, me_seq),
            send_sem=in_send.at[which, 0], recv_sem=in_recv.at[which, item],
            device_id=chip(group, x_side, local // 2), device_id_type=MESH,
        )

    def shared_block(which, step):
        group = group_at(step)
        return pltpu.make_async_remote_copy(
            src_ref=ins.at[which, 3 * group + 2],
            dst_ref=place(which, item_slot(which, 2), me_seq),
            send_sem=in_send.at[which, 1], recv_sem=in_recv.at[which, 2],
            device_id=chip(group, local // 2, lax.rem(local, 2)), device_id_type=MESH,
        )

    major_home = local // 2 == core
    shared_home = local // 2 == side

    def start_major(which):
        item = lax.rem(local, 2)
        slot = item if which == 0 else 1 + item

        @pl.when(major_home)
        def _():
            pltpu.make_async_copy(
                ins.at[which, 3 * me_group + side],
                place(which, slot, me_seq),
                in_recv.at[which, item],
            ).start()

        @pl.when(jnp.logical_not(major_home))
        def _():
            major_block(which, 0, side).start()

        major_block(which, 0, 1 - side).start()

        @pl.loop(1, 16)
        def _(step):
            major_block(which, step, side).start()
            major_block(which, step, 1 - side).start()

    def start_shared(which):
        @pl.when(shared_home)
        def _():
            pltpu.make_async_copy(
                ins.at[which, 3 * me_group + 2],
                place(which, item_slot(which, 2), me_seq),
                in_recv.at[which, 2],
            ).start()

        @pl.when(jnp.logical_not(shared_home))
        def _():
            shared_block(which, 0).start()

        @pl.loop(1, 16)
        def _(step):
            shared_block(which, step).start()

    def wait_item(which, item):
        ref = slot_ref(which, item_slot(which, item))
        pltpu.make_async_copy(ref, ref, in_recv.at[which, item]).wait()

    next_row = lax.rem(row + 1, 4)
    fwd_span = jnp.where(core == 0, me_span + 1, next_row * 4 + plane * 2)
    shared_row = jnp.where(side == 0, row, next_row)
    fwd_shared_span = jnp.where(core == 0, me_span + 1, shared_row * 4 + plane * 2)
    fwd_shared_seq = jnp.where(core == 0, me_seq, jnp.where(side == 0, me_seq + 1, me_seq - 1))
    last_row = row == 3
    fwd_major_sends = jnp.logical_not(jnp.logical_and(core == 1, last_row))
    fwd_shared_sends = jnp.logical_not(
        jnp.logical_and(jnp.logical_and(core == 1, side == 1), last_row)
    )
    first_row = jnp.logical_and(core == 0, row == 0)
    major_first = first_row
    shared_first = jnp.logical_and(first_row, side == 0)

    def forward(which, shared):
        return pltpu.make_async_remote_copy(
            src_ref=slot_ref(which, 4 if shared else 2),
            dst_ref=slot_ref(which, 3 if shared else 0),
            send_sem=fwd_send.at[which - 1, shared], recv_sem=fwd_recv.at[which - 1, shared],
            device_id=(fwd_shared_span, fwd_shared_seq) if shared else (fwd_span, me_seq),
            device_id_type=MESH,
        )

    def vis_block(offset):
        return pltpu.make_async_remote_copy(
            src_ref=vis_in, dst_ref=vis.at[local],
            send_sem=vis_send, recv_sem=vis_recv,
            device_id=(row * 4 + lax.rem(local + offset, 4), me_seq), device_id_type=MESH,
        )

    loads = [
        pltpu.make_async_copy(raw, loaded.at[which], load.at[which])
        for which, raw in enumerate((q_raw, k_raw, v_raw))
    ]
    for which in (1, 2, 0):
        loads[which].start()

    barrier = pltpu.get_barrier_semaphore()

    @pl.loop(1, 64)
    def _(step):
        other = lax.rem(local * 16 + me_seq + step, 64)
        pl.semaphore_signal(
            barrier, inc=1, device_id=(row * 4 + other // 16, lax.rem(other, 16)),
            device_id_type=MESH,
        )

    row_before = lax.rem(row + 3, 4) * 4 + plane * 2 + 1

    @pl.when(core == 0)
    def _():
        pl.semaphore_signal(
            barrier, inc=1, device_id=(row_before, me_seq), device_id_type=MESH
        )

    @pl.when(jnp.logical_and(core == 0, side == 0))
    def _():
        pl.semaphore_signal(
            barrier, inc=1, device_id=(row_before, me_seq + 1), device_id_type=MESH
        )

    column = lax.broadcasted_iota(jnp.int32, (TILES, TILE), 1)
    diagonal = lax.broadcasted_iota(jnp.int32, (TILES, TILES), 0) == lax.broadcasted_iota(
        jnp.int32, (TILES, TILES), 1
    )
    count = jnp.sum(
        jnp.where(diagonal, count_in[...].astype(jnp.float32), 0.0), axis=1, keepdims=True
    )
    seen = jnp.zeros((TILES, TILE), jnp.float32)
    for slot in range(2 * TILES):
        named = jnp.logical_and(list_in[:, slot:slot + 1] == column, count > slot)
        seen = jnp.where(named, 1.0, seen)
    vis_in[...] = seen

    for which in (1, 2, 0):
        loads[which].wait()
        ins[which] = jnp.transpose(loaded[which], (1, 0, 2))
        if which == 2:
            @pl.loop(0, HEADS // 4)
            def _(four):
                for part in range(4):
                    ins[2, 4 * four + part] = jnp.transpose(ins[2, 4 * four + part])

    pl.semaphore_wait(barrier, 63 + core * (1 + side))

    for offset in range(1, 4):
        vis_block(offset).start()
    pltpu.make_async_copy(vis_in, vis.at[local], vis_recv).start()
    for which in (1, 2):
        start_shared(which)
    start_major(1)

    @pl.when(major_first)
    def _():
        kb[:TOKENS, :] = jnp.zeros((TOKENS, WIDTH), jnp.bfloat16)
        vb[:, :TOKENS] = jnp.zeros((WIDTH, TOKENS), jnp.bfloat16)

    @pl.when(shared_first)
    def _():
        kb[3 * TOKENS:4 * TOKENS, :] = jnp.zeros((TOKENS, WIDTH), jnp.bfloat16)
        vb[:, 3 * TOKENS:4 * TOKENS] = jnp.zeros((WIDTH, TOKENS), jnp.bfloat16)

    pltpu.make_async_copy(vis, vis, vis_recv).wait()
    tile_of = lax.broadcasted_iota(jnp.int32, (TILES, TOKENS), 1) // TILE
    pick = (tile_of == lax.broadcasted_iota(jnp.int32, (TILES, TOKENS), 0)).astype(jnp.bfloat16)
    for item in range(PER):
        seen = matmul(vis[item_spans[item]].astype(jnp.bfloat16), pick, CONTRACT_FIRST)
        bias[item] = (1.0 - seen[:2 * TILES]) * HIDDEN

    def attend(item):
        shared = item == 2
        origin = pl.multiple_of(jnp.where(shared, 3, item) * TOKENS, TOKENS)
        item_span = jnp.where(shared, 2 * side + core, 2 * core + item)
        item_head = 3 * me_group + jnp.where(shared, 2, side)

        def block_result(block):
            columns = slice(block * QB, (block + 1) * QB)
            query = qb[pl.ds(pl.multiple_of(item * TOKENS + block * QB, QB), QB), :]
            held = scores.at[block % 2]
            keys_seen = TOKENS + (block + 1) * QB

            def hidden(tile):
                return bias[item, tile:tile + 1, columns]

            largest = jnp.full((8, QB), -3e38, jnp.float32)
            for first in range(0, keys_seen, KB):
                part = matmul(kb[pl.ds(origin + first, KB), :], query, CONTRACT_LAST)
                held[first:first + KB, :] = part
                for at in range(0, KB, TILE):
                    rows = part[at:at + TILE].reshape(TILE // 8, 8, QB)
                    largest = jnp.maximum(
                        largest, jnp.max(rows, axis=0) + hidden((first + at) // TILE)
                    )
            top = jnp.max(largest, axis=0, keepdims=True) * SCALE

            total = jnp.zeros((WIDTH, QB), jnp.float32)
            summed = jnp.zeros((8, QB), jnp.float32)
            for first in range(0, keys_seen, KB):
                parts = []
                for at in range(first, first + KB, TILE):
                    weight = jnp.exp2(held[at:at + TILE, :] * SCALE - (top - hidden(at // TILE)))
                    summed = summed + jnp.sum(weight.reshape(TILE // 8, 8, QB), axis=0)
                    parts.append(weight.astype(jnp.bfloat16))
                weights = jnp.concatenate(parts, 0)
                total = total + matmul(
                    vb[:, pl.ds(pl.multiple_of(origin + first, KB), KB)], weights, CONTRACT_PLAIN
                )
            result = total / jnp.sum(summed, axis=0, keepdims=True)
            ob[item, columns, :] = jnp.transpose(result).astype(jnp.bfloat16)

        for block in range(TOKENS // QB):
            block_result(block)

            @pl.loop(block * (QB // TILE), (block + 1) * (QB // TILE))
            def _(tile):
                source = ob.at[item, pl.ds(pl.multiple_of(tile * TILE, TILE), TILE), :]
                here = jnp.logical_and(item_span == local, tile == me_seq)

                @pl.when(here)
                def _():
                    pltpu.make_async_copy(source, arrived.at[item_head], o_recv).start()

                @pl.when(jnp.logical_not(here))
                def _():
                    pltpu.make_async_remote_copy(
                        src_ref=source, dst_ref=arrived.at[item_head],
                        send_sem=o_send.at[item], recv_sem=o_recv,
                        device_id=(row * 4 + item_span, tile), device_id_type=MESH,
                    ).start()

    for which in (1, 2):
        wait_item(which, 2)

        @pl.when(fwd_shared_sends)
        def _():
            forward(which, 1).start()

    start_major(2)

    wait_item(1, 1)

    @pl.when(fwd_major_sends)
    def _():
        forward(1, 0).start()

    start_major(0)
    wait_item(2, 1)

    @pl.when(fwd_major_sends)
    def _():
        forward(2, 0).start()

    start_shared(0)
    for which in (1, 2, 0):
        wait_item(which, 0)

    @pl.when(jnp.logical_not(major_first))
    def _():
        for which in (1, 2):
            ref = slot_ref(which, 0)
            pltpu.make_async_copy(ref, ref, fwd_recv.at[which - 1, 0]).wait()

    wait_item(0, 1)

    @pl.loop(0, PER)
    def _(item):
        @pl.when(item == 2)
        def _():
            wait_item(0, 2)

            @pl.when(jnp.logical_not(shared_first))
            def _():
                for which in (1, 2):
                    ref = slot_ref(which, 3)
                    pltpu.make_async_copy(ref, ref, fwd_recv.at[which - 1, 1]).wait()

        attend(item)

    pltpu.make_async_copy(arrived, arrived, o_recv).wait()

    for offset in range(1, 4):
        vis_block(offset).wait_send()
    for which in (0, 1, 2):
        sent = ins.at[which, :31]
        pltpu.make_async_copy(sent, sent, in_send.at[which, 0]).wait()
        sent = ins.at[which, :15]
        pltpu.make_async_copy(sent, sent, in_send.at[which, 1]).wait()

        @pl.when(jnp.logical_not(major_home))
        def _():
            major_block(which, 0, side).wait_send()

        @pl.when(jnp.logical_not(shared_home))
        def _():
            shared_block(which, 0).wait_send()

    @pl.when(fwd_major_sends)
    def _():
        for which in (1, 2):
            forward(which, 0).wait_send()

    @pl.when(fwd_shared_sends)
    def _():
        for which in (1, 2):
            forward(which, 1).wait_send()

    for item in range(PER):
        sent = arrived.at[:15]
        pltpu.make_async_copy(sent, sent, o_send.at[item]).wait()

        @pl.when(item_spans[item] != local)
        def _():
            last = arrived.at[0]
            pltpu.make_async_copy(last, last, o_send.at[item]).wait()


def by_token(by_head, out):
    out[...] = jnp.transpose(by_head[...], (1, 0, 2))


def per_device(query, keys, values, block_list, block_count):
    anywhere = pl.BlockSpec(memory_space=pl.ANY)
    vmem = pl.BlockSpec(memory_space=pltpu.VMEM)
    by_head = pl.pallas_call(
        kernel,
        out_shape=jax.ShapeDtypeStruct((HEADS, TILE, WIDTH), jnp.bfloat16),
        in_specs=[anywhere, anywhere, anywhere, vmem, vmem],
        out_specs=anywhere,
        scratch_shapes=[
            pltpu.VMEM((3, TILE, HEADS, WIDTH), jnp.bfloat16),
            pltpu.VMEM((3, HEADS, TILE, WIDTH), jnp.bfloat16),
            pltpu.VMEM((TILES, TILE), jnp.float32),
            pltpu.VMEM((PER * TOKENS, WIDTH), jnp.bfloat16),
            pltpu.VMEM((5 * TOKENS, WIDTH), jnp.bfloat16),
            pltpu.VMEM((WIDTH, 5 * TOKENS), jnp.bfloat16),
            pltpu.VMEM((PER, TOKENS, WIDTH), jnp.bfloat16),
            pltpu.VMEM((4, TILES, TILE), jnp.float32),
            pltpu.VMEM((PER, 2 * TILES, TOKENS), jnp.float32),
            pltpu.VMEM((2, 2 * TOKENS, QB), jnp.float32),
            pltpu.SemaphoreType.DMA((3,)),
            pltpu.SemaphoreType.DMA((3, 2)),
            pltpu.SemaphoreType.DMA((3, PER)),
            pltpu.SemaphoreType.DMA,
            pltpu.SemaphoreType.DMA,
            pltpu.SemaphoreType.DMA((2, 2)),
            pltpu.SemaphoreType.DMA((2, 2)),
            pltpu.SemaphoreType.DMA((PER,)),
            pltpu.SemaphoreType.DMA,
        ],
        compiler_params=pltpu.CompilerParams(
            vmem_limit_bytes=56 << 20, has_side_effects=True, collective_id=0
        ),
        name="exchange_and_attend",
    )(query[0], keys[0], values[0], block_list[0], block_count)
    rows = TILE // 2
    return pl.pallas_call(
        by_token,
        grid=(2,),
        out_shape=jax.ShapeDtypeStruct((TILE, HEADS, WIDTH), jnp.bfloat16),
        in_specs=[pl.BlockSpec((HEADS, rows, WIDTH), lambda i: (0, i, 0))],
        out_specs=pl.BlockSpec((rows, HEADS, WIDTH), lambda i: (i, 0, 0)),
        name="by_token",
    )(by_head)[None]


def solution(mesh):
    in_specs = (
        P("span", "seq", None, None),
        P("span", "seq", None, None),
        P("span", "seq", None, None),
        P("span", None, None),
        P("span", None),
    )
    out_specs = P("span", "seq", None, None)
    return jax.shard_map(
        per_device, mesh=mesh, in_specs=in_specs, out_specs=out_specs, check_vma=False
    )
```

```python
import functools
import math

import jax
import jax.numpy as jnp
from jax import lax
from jax.experimental import pallas as pl
from jax.experimental.pallas import tpu as pltpu
from jax.sharding import PartitionSpec as P

MESH = pl.DeviceIdType.MESH
TILE = 128
TILES = 16
TOKENS = TILE * TILES
SPANS = 16
SEQ = 16
HEADS = 48
PER = HEADS // SEQ
WIDTH = 128
QB = 256
KB = 256
SCALE = math.log2(math.e) / math.sqrt(WIDTH)
HIDDEN = -1e30
CONTRACT_LAST = (((1,), (1,)), ((), ()))
CONTRACT_FIRST = (((0,), (0,)), ((), ()))
CONTRACT_PLAIN = (((1,), (0,)), ((), ()))


def matmul(left, right, dims):
    return lax.dot_general(left, right, dims, preferred_element_type=jnp.float32)


def kernel(
    q_raw, k_raw, v_raw, list_in, count_in, arrived,
    loaded, ins, vis_in, qb, kb, vb, ob, vis, bias, scores, load,
    in_send, in_recv, vis_send, vis_recv, fwd_send, fwd_recv, o_send, o_recv,
):
    me_span = lax.axis_index("span")
    me_seq = lax.axis_index("seq")
    row = me_span // 4
    local = lax.rem(me_span, 4)
    core = lax.rem(me_span, 2)
    plane = lax.rem(me_span // 2, 2)
    x = lax.rem(me_seq, 4)
    side = lax.rem(x, 2)
    z = me_seq // 4 * 2 + plane
    me_group = x // 2 * 8 + z
    item_spans = (2 * core, 2 * core + 1, 2 * side + core)

    base = (0, 1, 3)

    def place(which, slot, tile):
        at = pl.ds(pl.multiple_of(slot * TOKENS + tile * TILE, TILE), TILE)
        if which == 0:
            return qb.at[at, :]
        if which == 1:
            return kb.at[at, :]
        return vb.at[:, at]

    def slot_ref(which, slot):
        at = pl.ds(slot * TOKENS, TOKENS)
        if which == 0:
            return qb.at[at, :]
        if which == 1:
            return kb.at[at, :]
        return vb.at[:, at]

    def item_slot(which, item):
        return item if which == 0 else base[item] + 1

    def group_at(step):
        turn = step // 2
        far = (turn + 1) // 2
        z_step = (lax.rem(turn, 2) * 2 * far - far) * (1 - 2 * side)
        return lax.rem(x // 2 + step, 2) * 8 + lax.rem(z + z_step + 8, 8)

    def chip(group, x_side, its_core):
        its_z = lax.rem(group, 8)
        return (
            row * 4 + lax.rem(its_z, 2) * 2 + its_core,
            its_z // 2 * 4 + group // 8 * 2 + x_side,
        )

    def major_block(which, step, x_side):
        group = group_at(step)
        item = lax.rem(local, 2)
        slot = item if which == 0 else 1 + item
        return pltpu.make_async_remote_copy(
            src_ref=ins.at[which, 3 * group + x_side],
            dst_ref=place(which, slot, me_seq),
            send_sem=in_send.at[which, 0], recv_sem=in_recv.at[which, item],
            device_id=chip(group, x_side, local // 2), device_id_type=MESH,
        )

    def shared_block(which, step):
        group = group_at(step)
        return pltpu.make_async_remote_copy(
            src_ref=ins.at[which, 3 * group + 2],
            dst_ref=place(which, item_slot(which, 2), me_seq),
            send_sem=in_send.at[which, 1], recv_sem=in_recv.at[which, 2],
            device_id=chip(group, local // 2, lax.rem(local, 2)), device_id_type=MESH,
        )

    major_home = local // 2 == core
    shared_home = local // 2 == side

    def start_major(which):
        item = lax.rem(local, 2)
        slot = item if which == 0 else 1 + item

        @pl.when(major_home)
        def _():
            pltpu.make_async_copy(
                ins.at[which, 3 * me_group + side],
                place(which, slot, me_seq),
                in_recv.at[which, item],
            ).start()

        @pl.when(jnp.logical_not(major_home))
        def _():
            major_block(which, 0, side).start()

        major_block(which, 0, 1 - side).start()

        @pl.loop(1, 16)
        def _(near):
            major_block(which, 16 - near, side).start()
            major_block(which, 16 - near, 1 - side).start()

    def start_shared(which):
        @pl.when(shared_home)
        def _():
            pltpu.make_async_copy(
                ins.at[which, 3 * me_group + 2],
                place(which, item_slot(which, 2), me_seq),
                in_recv.at[which, 2],
            ).start()

        @pl.when(jnp.logical_not(shared_home))
        def _():
            shared_block(which, 0).start()

        @pl.loop(1, 16)
        def _(near):
            shared_block(which, 16 - near).start()

    def wait_item(which, item):
        ref = slot_ref(which, item_slot(which, item))
        pltpu.make_async_copy(ref, ref, in_recv.at[which, item]).wait()

    next_row = lax.rem(row + 1, 4)
    fwd_span = jnp.where(core == 0, me_span + 1, next_row * 4 + plane * 2)
    shared_row = jnp.where(side == 0, row, next_row)
    fwd_shared_span = jnp.where(core == 0, me_span + 1, shared_row * 4 + plane * 2)
    fwd_shared_seq = jnp.where(core == 0, me_seq, jnp.where(side == 0, me_seq + 1, me_seq - 1))
    last_row = row == 3
    fwd_major_sends = jnp.logical_not(jnp.logical_and(core == 1, last_row))
    fwd_shared_sends = jnp.logical_not(
        jnp.logical_and(jnp.logical_and(core == 1, side == 1), last_row)
    )
    first_row = jnp.logical_and(core == 0, row == 0)
    major_first = first_row
    shared_first = jnp.logical_and(first_row, side == 0)

    def forward(which, shared):
        return pltpu.make_async_remote_copy(
            src_ref=slot_ref(which, 4 if shared else 2),
            dst_ref=slot_ref(which, 3 if shared else 0),
            send_sem=fwd_send.at[which - 1, shared], recv_sem=fwd_recv.at[which - 1, shared],
            device_id=(fwd_shared_span, fwd_shared_seq) if shared else (fwd_span, me_seq),
            device_id_type=MESH,
        )

    def vis_block(offset):
        return pltpu.make_async_remote_copy(
            src_ref=vis_in, dst_ref=vis.at[local],
            send_sem=vis_send, recv_sem=vis_recv,
            device_id=(row * 4 + lax.rem(local + offset, 4), me_seq), device_id_type=MESH,
        )

    loads = [
        pltpu.make_async_copy(raw, loaded.at[which], load.at[which])
        for which, raw in enumerate((q_raw, k_raw, v_raw))
    ]
    for which in (1, 2, 0):
        loads[which].start()

    barrier = pltpu.get_barrier_semaphore()

    @pl.loop(1, 64)
    def _(step):
        other = lax.rem(local * 16 + me_seq + step, 64)
        pl.semaphore_signal(
            barrier, inc=1, device_id=(row * 4 + other // 16, lax.rem(other, 16)),
            device_id_type=MESH,
        )

    row_before = lax.rem(row + 3, 4) * 4 + plane * 2 + 1

    @pl.when(core == 0)
    def _():
        pl.semaphore_signal(
            barrier, inc=1, device_id=(row_before, me_seq), device_id_type=MESH
        )

    @pl.when(jnp.logical_and(core == 0, side == 0))
    def _():
        pl.semaphore_signal(
            barrier, inc=1, device_id=(row_before, me_seq + 1), device_id_type=MESH
        )

    column = lax.broadcasted_iota(jnp.int32, (TILES, TILE), 1)
    diagonal = lax.broadcasted_iota(jnp.int32, (TILES, TILES), 0) == lax.broadcasted_iota(
        jnp.int32, (TILES, TILES), 1
    )
    count = jnp.sum(
        jnp.where(diagonal, count_in[...].astype(jnp.float32), 0.0), axis=1, keepdims=True
    )
    seen = jnp.zeros((TILES, TILE), jnp.float32)
    for slot in range(2 * TILES):
        named = jnp.logical_and(list_in[:, slot:slot + 1] == column, count > slot)
        seen = jnp.where(named, 1.0, seen)
    vis_in[...] = seen

    for which in (1, 2, 0):
        loads[which].wait()
        ins[which] = jnp.transpose(loaded[which], (1, 0, 2))
        if which == 2:
            @pl.loop(0, HEADS // 4)
            def _(four):
                for part in range(4):
                    ins[2, 4 * four + part] = jnp.transpose(ins[2, 4 * four + part])

    pl.semaphore_wait(barrier, 63 + core * (1 + side))

    for offset in range(1, 4):
        vis_block(offset).start()
    pltpu.make_async_copy(vis_in, vis.at[local], vis_recv).start()
    for which in (1, 2):
        start_shared(which)
    start_major(1)

    @pl.when(major_first)
    def _():
        kb[:TOKENS, :] = jnp.zeros((TOKENS, WIDTH), jnp.bfloat16)
        vb[:, :TOKENS] = jnp.zeros((WIDTH, TOKENS), jnp.bfloat16)

    @pl.when(shared_first)
    def _():
        kb[3 * TOKENS:4 * TOKENS, :] = jnp.zeros((TOKENS, WIDTH), jnp.bfloat16)
        vb[:, 3 * TOKENS:4 * TOKENS] = jnp.zeros((WIDTH, TOKENS), jnp.bfloat16)

    pltpu.make_async_copy(vis, vis, vis_recv).wait()
    tile_of = lax.broadcasted_iota(jnp.int32, (TILES, TOKENS), 1) // TILE
    pick = (tile_of == lax.broadcasted_iota(jnp.int32, (TILES, TOKENS), 0)).astype(jnp.bfloat16)
    for item in range(PER):
        seen = matmul(vis[item_spans[item]].astype(jnp.bfloat16), pick, CONTRACT_FIRST)
        bias[item] = (1.0 - seen[:2 * TILES]) * HIDDEN

    def attend(item):
        shared = item == 2
        origin = pl.multiple_of(jnp.where(shared, 3, item) * TOKENS, TOKENS)
        item_span = jnp.where(shared, 2 * side + core, 2 * core + item)
        item_head = 3 * me_group + jnp.where(shared, 2, side)

        def block_result(block):
            columns = slice(block * QB, (block + 1) * QB)
            query = qb[pl.ds(pl.multiple_of(item * TOKENS + block * QB, QB), QB), :]
            held = scores.at[block % 2]
            keys_seen = TOKENS + (block + 1) * QB

            def hidden(tile):
                return bias[item, tile:tile + 1, columns]

            largest = jnp.full((8, QB), -3e38, jnp.float32)
            for first in range(0, keys_seen, KB):
                part = matmul(kb[pl.ds(origin + first, KB), :], query, CONTRACT_LAST)
                held[first:first + KB, :] = part
                for at in range(0, KB, TILE):
                    rows = part[at:at + TILE].reshape(TILE // 8, 8, QB)
                    largest = jnp.maximum(
                        largest, jnp.max(rows, axis=0) + hidden((first + at) // TILE)
                    )
            top = jnp.max(largest, axis=0, keepdims=True) * SCALE

            total = jnp.zeros((WIDTH, QB), jnp.float32)
            summed = jnp.zeros((8, QB), jnp.float32)
            for first in range(0, keys_seen, KB):
                parts = []
                for at in range(first, first + KB, TILE):
                    weight = jnp.exp2(held[at:at + TILE, :] * SCALE - (top - hidden(at // TILE)))
                    summed = summed + jnp.sum(weight.reshape(TILE // 8, 8, QB), axis=0)
                    parts.append(weight.astype(jnp.bfloat16))
                weights = jnp.concatenate(parts, 0)
                total = total + matmul(
                    vb[:, pl.ds(pl.multiple_of(origin + first, KB), KB)], weights, CONTRACT_PLAIN
                )
            result = total / jnp.sum(summed, axis=0, keepdims=True)
            ob[item, columns, :] = jnp.transpose(result).astype(jnp.bfloat16)

        for block in range(TOKENS // QB):
            block_result(block)

            @pl.loop(block * (QB // TILE), (block + 1) * (QB // TILE))
            def _(tile):
                source = ob.at[item, pl.ds(pl.multiple_of(tile * TILE, TILE), TILE), :]
                here = jnp.logical_and(item_span == local, tile == me_seq)

                @pl.when(here)
                def _():
                    pltpu.make_async_copy(source, arrived.at[item_head], o_recv).start()

                @pl.when(jnp.logical_not(here))
                def _():
                    pltpu.make_async_remote_copy(
                        src_ref=source, dst_ref=arrived.at[item_head],
                        send_sem=o_send.at[item], recv_sem=o_recv,
                        device_id=(row * 4 + item_span, tile), device_id_type=MESH,
                    ).start()

    for which in (1, 2):
        wait_item(which, 2)

        @pl.when(fwd_shared_sends)
        def _():
            forward(which, 1).start()

    start_major(2)

    wait_item(1, 1)

    @pl.when(fwd_major_sends)
    def _():
        forward(1, 0).start()

    start_major(0)
    wait_item(2, 1)

    @pl.when(fwd_major_sends)
    def _():
        forward(2, 0).start()

    start_shared(0)
    for which in (1, 2, 0):
        wait_item(which, 0)

    @pl.when(jnp.logical_not(major_first))
    def _():
        for which in (1, 2):
            ref = slot_ref(which, 0)
            pltpu.make_async_copy(ref, ref, fwd_recv.at[which - 1, 0]).wait()

    wait_item(0, 1)

    @pl.loop(0, PER)
    def _(item):
        @pl.when(item == 2)
        def _():
            wait_item(0, 2)

            @pl.when(jnp.logical_not(shared_first))
            def _():
                for which in (1, 2):
                    ref = slot_ref(which, 3)
                    pltpu.make_async_copy(ref, ref, fwd_recv.at[which - 1, 1]).wait()

        attend(item)

    pltpu.make_async_copy(arrived, arrived, o_recv).wait()

    for offset in range(1, 4):
        vis_block(offset).wait_send()
    for which in (0, 1, 2):
        sent = ins.at[which, :31]
        pltpu.make_async_copy(sent, sent, in_send.at[which, 0]).wait()
        sent = ins.at[which, :15]
        pltpu.make_async_copy(sent, sent, in_send.at[which, 1]).wait()

        @pl.when(jnp.logical_not(major_home))
        def _():
            major_block(which, 0, side).wait_send()

        @pl.when(jnp.logical_not(shared_home))
        def _():
            shared_block(which, 0).wait_send()

    @pl.when(fwd_major_sends)
    def _():
        for which in (1, 2):
            forward(which, 0).wait_send()

    @pl.when(fwd_shared_sends)
    def _():
        for which in (1, 2):
            forward(which, 1).wait_send()

    for item in range(PER):
        sent = arrived.at[:15]
        pltpu.make_async_copy(sent, sent, o_send.at[item]).wait()

        @pl.when(item_spans[item] != local)
        def _():
            last = arrived.at[0]
            pltpu.make_async_copy(last, last, o_send.at[item]).wait()


def by_token(by_head, out):
    out[...] = jnp.transpose(by_head[...], (1, 0, 2))


def per_device(query, keys, values, block_list, block_count):
    anywhere = pl.BlockSpec(memory_space=pl.ANY)
    vmem = pl.BlockSpec(memory_space=pltpu.VMEM)
    by_head = pl.pallas_call(
        kernel,
        out_shape=jax.ShapeDtypeStruct((HEADS, TILE, WIDTH), jnp.bfloat16),
        in_specs=[anywhere, anywhere, anywhere, vmem, vmem],
        out_specs=anywhere,
        scratch_shapes=[
            pltpu.VMEM((3, TILE, HEADS, WIDTH), jnp.bfloat16),
            pltpu.VMEM((3, HEADS, TILE, WIDTH), jnp.bfloat16),
            pltpu.VMEM((TILES, TILE), jnp.float32),
            pltpu.VMEM((PER * TOKENS, WIDTH), jnp.bfloat16),
            pltpu.VMEM((5 * TOKENS, WIDTH), jnp.bfloat16),
            pltpu.VMEM((WIDTH, 5 * TOKENS), jnp.bfloat16),
            pltpu.VMEM((PER, TOKENS, WIDTH), jnp.bfloat16),
            pltpu.VMEM((4, TILES, TILE), jnp.float32),
            pltpu.VMEM((PER, 2 * TILES, TOKENS), jnp.float32),
            pltpu.VMEM((2, 2 * TOKENS, QB), jnp.float32),
            pltpu.SemaphoreType.DMA((3,)),
            pltpu.SemaphoreType.DMA((3, 2)),
            pltpu.SemaphoreType.DMA((3, PER)),
            pltpu.SemaphoreType.DMA,
            pltpu.SemaphoreType.DMA,
            pltpu.SemaphoreType.DMA((2, 2)),
            pltpu.SemaphoreType.DMA((2, 2)),
            pltpu.SemaphoreType.DMA((PER,)),
            pltpu.SemaphoreType.DMA,
        ],
        compiler_params=pltpu.CompilerParams(
            vmem_limit_bytes=56 << 20, has_side_effects=True, collective_id=0
        ),
        name="exchange_and_attend",
    )(query[0], keys[0], values[0], block_list[0], block_count)
    rows = TILE // 2
    return pl.pallas_call(
        by_token,
        grid=(2,),
        out_shape=jax.ShapeDtypeStruct((TILE, HEADS, WIDTH), jnp.bfloat16),
        in_specs=[pl.BlockSpec((HEADS, rows, WIDTH), lambda i: (0, i, 0))],
        out_specs=pl.BlockSpec((rows, HEADS, WIDTH), lambda i: (i, 0, 0)),
        name="by_token",
    )(by_head)[None]


def solution(mesh):
    in_specs = (
        P("span", "seq", None, None),
        P("span", "seq", None, None),
        P("span", "seq", None, None),
        P("span", None, None),
        P("span", None),
    )
    out_specs = P("span", "seq", None, None)
    return jax.shard_map(
        per_device, mesh=mesh, in_specs=in_specs, out_specs=out_specs, check_vma=False
    )
```
